512 devices in a mesh: leaf: 32 (over z, x), col: 16 (over y, core).
Axes of the slice: x: 4, y: 8, z: 8, core: 2. Of those that a mesh axis runs over, the one named last changes fastest.
Arguments:
- root_inverse: float32 [2048, 8, 256], P('leaf', None, 'col'), as said below
- panel: float32 [384, 4, 256, 256], P('leaf', None, 'col')
- diag_inverse: float32 [384, 256, 256], P('leaf'), as said below
- tile_rows: int32 [384, 4], P('leaf'), may hold values from 0 to 7, as said below
Outputs:
- root_variance: float32 [8, 256], P(None, 'col')
- covariance: float32 [384, 4, 256, 256], P('leaf', None, 'col')
- variance: float32 [384, 256], P('leaf')
The draws below stay inside these ranges and needn't reach their ends.
Inputs may be any that keep to these rules, and one draw needn't show every extreme that they name: `tile_rows`: each row lists 4 different root tiles in rising order, the last being 7. `root_inverse`: lower triangular with a positive diagonal, in the column order of the steps. `diag_inverse`: each block lower triangular with a positive diagonal.
All inputs are finite; a program needn't handle non-finite values.
Results may differ from the reference program's by a relative error of at most 0.000078.
Values sent between devices are 32-bit elements; how exact they have to be, the bound alone decides.
No kernel may reach another device: no remote copies, remote signals or barrier semaphores. Data moves between devices by JAX's collectives and lax.ppermute only.
A program may use at most 64 MiB of HBM per device.

```python
import jax
import jax.numpy as jnp
from jax import lax

TILE = 256
ROOT = 2048
KS = 4
ROOT_TILES = 8
CHILDREN = 384


def tile_layout_mask(key):
    random_base_key = jax.random.fold_in(key, 11)
    others = ROOT_TILES - 1
    picks = jax.random.randint(random_base_key, (CHILDREN, others), 0, 1 << 20)
    tile_ids = jnp.arange(others, dtype=jnp.int32)
    scores = (picks + tile_ids[None, :] * (1 << 17)) * ROOT_TILES + tile_ids[None, :]
    chosen = lax_top(scores, KS - 1)
    last_tile = jnp.full((CHILDREN, 1), ROOT_TILES - 1, dtype=jnp.int32)
    return jnp.sort(jnp.concatenate([chosen.astype(jnp.int32), last_tile], axis=1), axis=1)


def lax_top(scores, count):
    return jax.lax.top_k(scores, count)[1]


def lower_factor(key, batch_shape, order):
    noise_key = jax.random.fold_in(key, 31)
    diag_key = jax.random.fold_in(key, 37)
    entries = jax.random.normal(noise_key, batch_shape + (order, order), jnp.float32)
    diagonal = jax.random.uniform(diag_key, batch_shape + (order,), jnp.float32, 0.6, 1.4)
    row_ids = jnp.arange(order)[:, None]
    col_ids = jnp.arange(order)[None, :]
    strict = jnp.where(row_ids > col_ids, entries * order ** (-0.5), 0.0)
    return strict + jnp.where(row_ids == col_ids, diagonal[..., None], 0.0)


def draw_root_inverse(key, part):
    return lower_factor(jax.random.fold_in(key, 41), (), ROOT).reshape(ROOT, ROOT_TILES, TILE)


def draw_diag_inverse(key, part):
    return lower_factor(jax.random.fold_in(key, 43), (CHILDREN,), TILE)


def draw_tile_rows(key, part):
    return tile_layout_mask(key)


def draw_panel(key, part):
    value_key = jax.random.fold_in(key, 23)
    entries = jax.random.normal(value_key, (CHILDREN, KS, TILE, TILE), jnp.float32)
    spread_factor = 2.0 * (KS * TILE) ** (-0.5)
    return entries * spread_factor


def setup_inputs(seed: int = 0) -> dict:
    arg_keys = jax.random.split(jax.random.key(seed), 5)
    return {
        "root_inverse": draw_root_inverse(jax.random.fold_in(arg_keys[4], 71), 0),
        "panel": draw_panel(jax.random.fold_in(arg_keys[4], 71), 0),
        "diag_inverse": draw_diag_inverse(jax.random.fold_in(arg_keys[4], 71), 0),
        "tile_rows": draw_tile_rows(jax.random.fold_in(arg_keys[4], 71), 0),
    }


def reference(root_inverse, panel, diag_inverse, tile_rows):
    highest_precision = lax.Precision.HIGHEST
    factor = root_inverse.reshape(ROOT, ROOT)
    sigma_root = jnp.dot(factor.T, factor, precision=highest_precision, preferred_element_type=jnp.float32)
    root_variance = jnp.diagonal(sigma_root).reshape(ROOT_TILES, TILE)
    lhat = jnp.einsum("ckot,cts->ckos", panel, diag_inverse, precision=highest_precision)
    offsets = jnp.arange(TILE, dtype=jnp.int32)
    rows = (tile_rows.astype(jnp.int32)[:, :, None] * TILE + offsets[None, None, :]).reshape(CHILDREN, KS * TILE)

    def one_child(item):
        rows_child, lhat_child = item
        block = jnp.take(jnp.take(sigma_root, rows_child, axis=0), rows_child, axis=1)
        return jnp.dot(block, lhat_child.reshape(KS * TILE, TILE), precision=highest_precision, preferred_element_type=jnp.float32)

    product = lax.map(one_child, (rows, lhat)).reshape(CHILDREN, KS, TILE, TILE)
    covariance = -product
    variance = jnp.sum(diag_inverse * diag_inverse, axis=1) - jnp.sum(lhat * covariance, axis=(1, 2))
    return root_variance, covariance, variance
```

```python
import functools

import jax
import jax.numpy as jnp
from jax import lax
from jax.experimental import pallas as pl
from jax.experimental.pallas import tpu as pltpu
from jax.sharding import PartitionSpec as P

F32 = jnp.float32
BF16 = jnp.bfloat16


def split(x):
    hi = x.astype(BF16)
    lo = (x - hi.astype(F32)).astype(BF16)
    return hi, lo


def mm(a, b):
    return jnp.dot(a, b, preferred_element_type=F32)


def product_kernel(rows_ref, col_ref, sig_ref, lfull_ref, lown_ref, cov_ref, term_ref, diag_ref, hi_ref, lo_ref):
    child = pl.program_id(0)
    tiles, width, depth = hi_ref.shape
    cls = width // tiles
    per_part = sig_ref.shape[3] // depth

    @pl.when(child == 0)
    def _():
        first = col_ref[0] * cls
        lane = lax.broadcasted_iota(jnp.int32, (cls, depth), 1)
        row = lax.broadcasted_iota(jnp.int32, (cls, depth), 0)
        on_diag = lane == row + first
        for p in range(tiles):
            part, place = divmod(p, per_part)
            block = sig_ref[:, part, :, place * depth : (place + 1) * depth].reshape(width, depth)
            hi, lo = split(block)
            hi_ref[p] = hi
            lo_ref[p] = lo
            own = block[p * cls : (p + 1) * cls]
            diag_ref[p : p + 1, :] = jnp.sum(jnp.where(on_diag, own, 0.0), axis=0, keepdims=True)

    listed = lfull_ref.shape[1]
    acc = None
    for p in range(listed):
        tp = rows_ref[child, p]
        picks = [pl.ds(pl.multiple_of(rows_ref[child, q] * cls, cls), cls) for q in range(listed)]
        shi = jnp.concatenate([hi_ref[tp, s, :] for s in picks], axis=0)
        slo = jnp.concatenate([lo_ref[tp, s, :] for s in picks], axis=0)
        lhi, llo = split(lfull_ref[0, p])
        term = mm(shi, lhi) + (mm(shi, llo) + mm(slo, lhi))
        acc = term if acc is None else acc + term
    cov = -acc
    cov_ref[0] = cov.reshape(cov_ref.shape[1:])
    own = lown_ref[0].reshape(cov.shape)
    term_ref[0] = jnp.sum(own * cov, axis=0, keepdims=True)


def product(tile_rows, col, sig, lfull, lown):
    children, listed, depth, out_width = lfull.shape
    cls = lown.shape[2]
    tiles = sig.shape[0] * sig.shape[2] // cls
    width = tiles * cls
    grid_spec = pltpu.PrefetchScalarGridSpec(
        num_scalar_prefetch=2,
        grid=(children,),
        in_specs=[
            pl.BlockSpec(sig.shape, lambda j, *_: (0, 0, 0, 0)),
            pl.BlockSpec((1, listed, depth, out_width), lambda j, *_: (j, 0, 0, 0)),
            pl.BlockSpec((1, listed, cls, out_width), lambda j, *_: (j, 0, 0, 0)),
        ],
        out_specs=[
            pl.BlockSpec((1, listed, cls, out_width), lambda j, *_: (j, 0, 0, 0)),
            pl.BlockSpec((1, 1, out_width), lambda j, *_: (j, 0, 0)),
            pl.BlockSpec((tiles, depth), lambda j, *_: (0, 0)),
        ],
        scratch_shapes=[
            pltpu.VMEM((tiles, width, depth), BF16),
            pltpu.VMEM((tiles, width, depth), BF16),
        ],
    )
    return pl.pallas_call(
        product_kernel,
        grid_spec=grid_spec,
        out_shape=[
            jax.ShapeDtypeStruct(lown.shape, F32),
            jax.ShapeDtypeStruct((children, 1, out_width), F32),
            jax.ShapeDtypeStruct((tiles, depth), F32),
        ],
        name="product",
    )(tile_rows, col, sig, lfull, lown)


def body(leaves, root_inverse, panel, diag_inverse, tile_rows):
    local_rows, tile_count, class_width = root_inverse.shape
    tile_width = panel.shape[3]
    width = tile_count * class_width
    root_order = tile_count * tile_width
    col_index = lax.axis_index("col")
    lhat = jnp.einsum(
        "ckot,cts->ckos", panel, diag_inverse, precision=lax.Precision.HIGHEST, preferred_element_type=F32
    )
    lfull = lax.all_gather(lhat, "col", axis=2, tiled=True)
    root_late, _ = lax.optimization_barrier((root_inverse, lhat))
    factor_rows = lax.all_gather(root_late, "col", axis=2, tiled=True).reshape(local_rows, root_order)
    partial = jnp.einsum(
        "rx,rk->xk",
        root_late.reshape(local_rows, width),
        factor_rows,
        precision=lax.Precision.HIGHEST,
        preferred_element_type=F32,
    )
    lines = 8
    parts = leaves * lines // width
    pieces = partial.reshape(width // lines, lines, parts, root_order // parts).transpose(0, 2, 1, 3)
    pieces = pieces.reshape(leaves, lines, root_order // parts)
    pieces = lax.all_to_all(pieces, "leaf", split_axis=0, concat_axis=0, tiled=True)
    own_piece = jnp.sum(pieces, axis=0)
    spread = jnp.broadcast_to(own_piece[None], pieces.shape)
    sig = lax.all_to_all(spread, "leaf", split_axis=0, concat_axis=0, tiled=True)
    sig = sig.reshape(width // lines, parts, lines, root_order // parts)
    covariance, terms, diag = product(tile_rows, col_index.reshape(1), sig, lfull, lhat)
    root_variance = lax.dynamic_slice_in_dim(diag, col_index * class_width, class_width, 1)
    all_terms = lax.all_gather(terms[:, 0, :], "col", axis=0)
    variance = jnp.sum(diag_inverse * diag_inverse, axis=1) - jnp.sum(all_terms, axis=0)
    return root_variance, covariance, variance


def solution(mesh):
    in_specs = (
        P("leaf", None, "col"),
        P("leaf", None, "col", None),
        P("leaf", None, None),
        P("leaf", None),
    )
    out_specs = (P(None, "col"), P("leaf", None, "col", None), P("leaf", None))
    return jax.shard_map(
        functools.partial(body, mesh.shape["leaf"]), mesh=mesh, in_specs=in_specs, out_specs=out_specs, check_vma=False
    )
```

```python
import jax
import jax.numpy as jnp
from jax import lax
from jax.experimental import pallas as pl
from jax.experimental.pallas import tpu as pltpu
from jax.sharding import Mesh
from jax.sharding import PartitionSpec as P

F32 = jnp.float32
BF16 = jnp.bfloat16
SCALE_STEP = 3
PRODUCT_STEP = 1


def split(x):
    hi = x.astype(BF16)
    lo = (x - hi.astype(F32)).astype(BF16)
    return hi, lo


def mm(a, b):
    return jnp.dot(a, b, preferred_element_type=F32)


def scale_kernel(panel_hbm, inverse_hbm, lhat_hbm, square_ref, panel_buf, inverse_buf, lhat_buf, panel_sem, inverse_sem, out_sem):
    children = inverse_buf.shape[0]
    rows = panel_buf.shape[1] * panel_buf.shape[2]

    def fetch(j):
        return (
            pltpu.make_async_copy(panel_hbm.at[j], panel_buf.at[j], panel_sem.at[j]),
            pltpu.make_async_copy(inverse_hbm.at[j], inverse_buf.at[j], inverse_sem.at[j]),
        )

    def drain(j):
        return pltpu.make_async_copy(lhat_buf.at[j], lhat_hbm.at[j], out_sem.at[j])

    @pl.loop(0, children)
    def _(j):
        for copy in fetch(j):
            copy.start()

    def one(j):
        inverse = inverse_buf[j]
        ihi, ilo = split(inverse)
        phi, plo = split(panel_buf[j].reshape(rows, inverse.shape[0]))
        both = mm(jnp.concatenate([phi, plo], axis=0), ihi)
        lhat = both[:rows] + (both[rows:] + mm(phi, ilo))
        lhat_buf[j] = lhat.reshape(lhat_buf.shape[1:])
        square_ref[pl.ds(j, 1), :] = jnp.sum(inverse * inverse, axis=0, keepdims=True)

    @pl.loop(0, children // SCALE_STEP)
    def _(i):
        group = [i * SCALE_STEP + u for u in range(SCALE_STEP)]
        for j in group:
            for copy in fetch(j):
                copy.wait()
        for j in group:
            one(j)
        for j in group:
            drain(j).start()

    @pl.loop(0, children)
    def _(j):
        drain(j).wait()


def scale(panel, inverse):
    children = inverse.shape[0]
    hbm = pl.BlockSpec(memory_space=pltpu.HBM)
    return pl.pallas_call(
        scale_kernel,
        in_specs=[hbm, hbm],
        out_specs=[hbm, pl.BlockSpec(memory_space=pltpu.VMEM)],
        out_shape=[
            jax.ShapeDtypeStruct(panel.shape, F32),
            jax.ShapeDtypeStruct((children, inverse.shape[2]), F32),
        ],
        scratch_shapes=[
            pltpu.VMEM(panel.shape, F32),
            pltpu.VMEM(inverse.shape, F32),
            pltpu.VMEM(panel.shape, F32),
            pltpu.SemaphoreType.DMA((children,)),
            pltpu.SemaphoreType.DMA((children,)),
            pltpu.SemaphoreType.DMA((children,)),
        ],
        name="scale",
    )(panel, inverse)


def prepare_kernel(col_ref, sig_ref, hi_ref, lo_ref, diag_ref):
    tiles, width, depth = hi_ref.shape
    cls = width // tiles
    per_part = sig_ref.shape[3] // depth
    first = col_ref[0] * cls
    lane = lax.broadcasted_iota(jnp.int32, (cls, depth), 1)
    row = lax.broadcasted_iota(jnp.int32, (cls, depth), 0)
    on_diag = lane == row + first
    for p in range(tiles):
        part, place = divmod(p, per_part)
        block = sig_ref[:, part, :, place * depth : (place + 1) * depth].reshape(width, depth)
        hi, lo = split(block)
        hi_ref[p] = hi
        lo_ref[p] = lo
        own = block[p * cls : (p + 1) * cls]
        diag_ref[p : p + 1, :] = jnp.sum(jnp.where(on_diag, own, 0.0), axis=0, keepdims=True)


def prepare(col, sig, tiles, depth):
    width = sig.shape[0] * sig.shape[2]
    vmem = pl.BlockSpec(memory_space=pltpu.VMEM)
    return pl.pallas_call(
        prepare_kernel,
        in_specs=[pl.BlockSpec(memory_space=pltpu.SMEM), vmem],
        out_specs=[vmem, vmem, vmem],
        out_shape=[
            jax.ShapeDtypeStruct((tiles, width, depth), BF16),
            jax.ShapeDtypeStruct((tiles, width, depth), BF16),
            jax.ShapeDtypeStruct((tiles, depth), F32),
        ],
        compiler_params=pltpu.CompilerParams(vmem_limit_bytes=8 << 20),
        name="prepare",
    )(col, sig)


def product_kernel(rows_ref, hi_ref, lo_ref, lown_ref, lfull_hbm, cov_hbm, term_ref, lfull_buf, cov_buf, in_sem, out_sem):
    children, listed, depth, out_width = lfull_buf.shape
    cls = lown_ref.shape[2]

    def fetch(j):
        return pltpu.make_async_copy(lfull_hbm.at[j], lfull_buf.at[j], in_sem.at[j])

    def drain(j):
        return pltpu.make_async_copy(cov_buf.at[j], cov_hbm.at[j], out_sem.at[j])

    @pl.loop(0, children)
    def _(j):
        fetch(j).start()

    def one(j):
        picks = [pl.ds(pl.multiple_of(rows_ref[j, q] * cls, cls), cls) for q in range(listed)]
        rows = listed * cls
        acc = None
        for p in range(listed):
            tp = rows_ref[j, p]
            both = jnp.concatenate([hi_ref[tp, s, :] for s in picks] + [lo_ref[tp, s, :] for s in picks], axis=0)
            lhi, llo = split(lfull_buf[j, p])
            first = mm(both, lhi)
            term = first[:rows] + (first[rows:] + mm(both[:rows], llo))
            acc = term if acc is None else acc + term
        cov = -acc
        cov_buf[j] = cov.reshape(cov_buf.shape[1:])
        own = lown_ref[j].reshape(cov.shape)
        term_ref[pl.ds(j, 1), :] = jnp.sum(own * cov, axis=0, keepdims=True)

    @pl.loop(0, children // PRODUCT_STEP)
    def _(i):
        group = [i * PRODUCT_STEP + u for u in range(PRODUCT_STEP)]
        for j in group:
            fetch(j).wait()
        for j in group:
            one(j)
        for j in group:
            drain(j).start()

    @pl.loop(0, children)
    def _(j):
        drain(j).wait()


def product(tile_rows, hi, lo, lfull, lown):
    children, listed, depth, out_width = lfull.shape
    vmem = pl.BlockSpec(memory_space=pltpu.VMEM)
    hbm = pl.BlockSpec(memory_space=pltpu.HBM)
    return pl.pallas_call(
        product_kernel,
        in_specs=[pl.BlockSpec(memory_space=pltpu.SMEM), vmem, vmem, vmem, hbm],
        out_specs=[hbm, vmem],
        out_shape=[
            jax.ShapeDtypeStruct(lown.shape, F32),
            jax.ShapeDtypeStruct((children, out_width), F32),
        ],
        scratch_shapes=[
            pltpu.VMEM(lfull.shape, F32),
            pltpu.VMEM(lown.shape, F32),
            pltpu.SemaphoreType.DMA((children,)),
            pltpu.SemaphoreType.DMA((children,)),
        ],
        compiler_params=pltpu.CompilerParams(vmem_limit_bytes=46 << 20),
        name="product",
    )(tile_rows, hi, lo, lown, lfull)


LEAF = {"z": 8, "x": 4}
COL = {"y": 8, "core": 2}


def exchange(value, axis):
    return lax.all_to_all(value, axis, split_axis=0, concat_axis=0, tiled=True)


def spread(value, axis, size):
    return exchange(jnp.broadcast_to(value[None], (size,) + value.shape), axis)


def body(root_inverse, panel, diag_inverse, tile_rows):
    local_rows, tile_count, class_width = root_inverse.shape
    tile_width = panel.shape[3]
    width = tile_count * class_width
    root_order = tile_count * tile_width
    z, x = LEAF["z"], LEAF["x"]
    col = tuple(COL)
    col_count = COL["y"] * COL["core"]
    col_index = lax.axis_index(col)
    lhat, squares = scale(panel, diag_inverse)
    lfull = lax.all_gather(lhat, col, axis=2, tiled=True)
    root_late, _ = lax.optimization_barrier((root_inverse, lhat))
    factor_rows = lax.all_gather(root_late, col, axis=2, tiled=True).reshape(local_rows, root_order)
    partial = jnp.einsum(
        "rx,rk->xk",
        root_late.reshape(local_rows, width),
        factor_rows,
        precision=lax.Precision.HIGHEST,
        preferred_element_type=F32,
    )
    lines = 8
    halves = z * x * lines // width
    half = root_order // halves
    strip = jnp.sum(exchange(partial.reshape(x, width // x, root_order), "x"), axis=0)
    pieces = strip.reshape(z // halves, lines, halves, half).transpose(0, 2, 1, 3).reshape(z, lines, half)
    piece = jnp.sum(exchange(pieces, "z"), axis=0)
    sig = spread(spread(piece, "z", z), "x", x)
    sig = sig.reshape(width // lines, halves, lines, half)
    hi, lo, diag = prepare(col_index.reshape(1), sig, tile_count, tile_width)
    root_variance = lax.dynamic_slice_in_dim(diag, col_index * class_width, class_width, 1)
    covariance, terms = product(tile_rows, hi, lo, lfull, lhat)
    variance = squares - jnp.sum(spread(terms, col, col_count), axis=0)
    return root_variance, covariance, variance


def solution(mesh):
    sizes = {**LEAF, **COL}
    fine = Mesh(mesh.devices.reshape(tuple(sizes.values())), tuple(sizes))
    leaf, col = tuple(LEAF), tuple(COL)
    in_specs = (P(leaf, None, col), P(leaf, None, col, None), P(leaf, None, None), P(leaf, None))
    out_specs = (P(None, col), P(leaf, None, col, None), P(leaf, None))
    return jax.shard_map(body, mesh=fine, in_specs=in_specs, out_specs=out_specs, check_vma=False)
```

```python
import jax
import jax.numpy as jnp
from jax import lax
from jax.experimental import pallas as pl
from jax.experimental.pallas import tpu as pltpu
from jax.sharding import Mesh
from jax.sharding import PartitionSpec as P

F32 = jnp.float32
BF16 = jnp.bfloat16
SCALE_STEP = 3
PRODUCT_STEP = 1


def split(x):
    hi = x.astype(BF16)
    lo = (x - hi.astype(F32)).astype(BF16)
    return hi, lo


def mm(a, b):
    return jnp.dot(a, b, preferred_element_type=F32)


def scale_kernel(panel_hbm, inverse_hbm, lhat_hbm, square_ref, panel_buf, inverse_buf, lhat_buf, panel_sem, inverse_sem, out_sem):
    children = inverse_buf.shape[0]
    rows = panel_buf.shape[1] * panel_buf.shape[2]

    def fetch(j):
        return (
            pltpu.make_async_copy(panel_hbm.at[j], panel_buf.at[j], panel_sem.at[j]),
            pltpu.make_async_copy(inverse_hbm.at[j], inverse_buf.at[j], inverse_sem.at[j]),
        )

    def drain(j):
        return pltpu.make_async_copy(lhat_buf.at[j], lhat_hbm.at[j], out_sem.at[j])

    @pl.loop(0, children)
    def _(j):
        for copy in fetch(j):
            copy.start()

    def one(j):
        inverse = inverse_buf[j]
        ihi, ilo = split(inverse)
        phi, plo = split(panel_buf[j].reshape(rows, inverse.shape[0]))
        both = mm(jnp.concatenate([phi, plo], axis=0), ihi)
        lhat = both[:rows] + (both[rows:] + mm(phi, ilo))
        lhat_buf[j] = lhat.reshape(lhat_buf.shape[1:])
        square_ref[pl.ds(j, 1), :] = jnp.sum(inverse * inverse, axis=0, keepdims=True)

    @pl.loop(0, children // SCALE_STEP)
    def _(i):
        group = [i * SCALE_STEP + u for u in range(SCALE_STEP)]
        for j in group:
            for copy in fetch(j):
                copy.wait()
        for j in group:
            one(j)
        for j in group:
            drain(j).start()

    @pl.loop(0, children)
    def _(j):
        drain(j).wait()


def scale(panel, inverse):
    children = inverse.shape[0]
    hbm = pl.BlockSpec(memory_space=pltpu.HBM)
    return pl.pallas_call(
        scale_kernel,
        in_specs=[hbm, hbm],
        out_specs=[hbm, pl.BlockSpec(memory_space=pltpu.VMEM)],
        out_shape=[
            jax.ShapeDtypeStruct(panel.shape, F32),
            jax.ShapeDtypeStruct((children, inverse.shape[2]), F32),
        ],
        scratch_shapes=[
            pltpu.VMEM(panel.shape, F32),
            pltpu.VMEM(inverse.shape, F32),
            pltpu.VMEM(panel.shape, F32),
            pltpu.SemaphoreType.DMA((children,)),
            pltpu.SemaphoreType.DMA((children,)),
            pltpu.SemaphoreType.DMA((children,)),
        ],
        name="scale",
    )(panel, inverse)


def prepare_kernel(col_ref, sig_ref, hi_ref, lo_ref, diag_ref):
    tiles, width, depth = hi_ref.shape
    cls = width // tiles
    share = sig_ref.shape[2] // depth
    first = col_ref[0] * cls
    lane = lax.broadcasted_iota(jnp.int32, (cls, depth), 1)
    row = lax.broadcasted_iota(jnp.int32, (cls, depth), 0)
    on_diag = lane == row + first
    for p in range(tiles):
        part, place = divmod(p, share)
        block = sig_ref[part, :, place * depth : (place + 1) * depth]
        hi, lo = split(block)
        hi_ref[p] = hi
        lo_ref[p] = lo
        own = block[p * cls : (p + 1) * cls]
        diag_ref[p : p + 1, :] = jnp.sum(jnp.where(on_diag, own, 0.0), axis=0, keepdims=True)


def prepare(col, sig, tiles, depth):
    width = sig.shape[1]
    vmem = pl.BlockSpec(memory_space=pltpu.VMEM)
    return pl.pallas_call(
        prepare_kernel,
        in_specs=[pl.BlockSpec(memory_space=pltpu.SMEM), vmem],
        out_specs=[vmem, vmem, vmem],
        out_shape=[
            jax.ShapeDtypeStruct((tiles, width, depth), BF16),
            jax.ShapeDtypeStruct((tiles, width, depth), BF16),
            jax.ShapeDtypeStruct((tiles, depth), F32),
        ],
        compiler_params=pltpu.CompilerParams(vmem_limit_bytes=8 << 20),
        name="prepare",
    )(col, sig)


def product_kernel(rows_ref, hi_ref, lo_ref, lown_ref, lfull_hbm, cov_hbm, term_ref, lfull_buf, cov_buf, in_sem, out_sem):
    children, listed, depth, out_width = lfull_buf.shape
    cls = lown_ref.shape[2]

    def fetch(j):
        return pltpu.make_async_copy(lfull_hbm.at[j], lfull_buf.at[j], in_sem.at[j])

    def drain(j):
        return pltpu.make_async_copy(cov_buf.at[j], cov_hbm.at[j], out_sem.at[j])

    @pl.loop(0, children)
    def _(j):
        fetch(j).start()

    def one(j):
        picks = [pl.ds(pl.multiple_of(rows_ref[j, q] * cls, cls), cls) for q in range(listed)]
        rows = listed * cls
        acc = None
        for p in range(listed):
            tp = rows_ref[j, p]
            both = jnp.concatenate([hi_ref[tp, s, :] for s in picks] + [lo_ref[tp, s, :] for s in picks], axis=0)
            lhi, llo = split(lfull_buf[j, p])
            first = mm(both, lhi)
            term = first[:rows] + (first[rows:] + mm(both[:rows], llo))
            acc = term if acc is None else acc + term
        cov = -acc
        cov_buf[j] = cov.reshape(cov_buf.shape[1:])
        own = lown_ref[j].reshape(cov.shape)
        term_ref[pl.ds(j, 1), :] = jnp.sum(own * cov, axis=0, keepdims=True)

    @pl.loop(0, children // PRODUCT_STEP)
    def _(i):
        group = [i * PRODUCT_STEP + u for u in range(PRODUCT_STEP)]
        for j in group:
            fetch(j).wait()
        for j in group:
            one(j)
        for j in group:
            drain(j).start()

    @pl.loop(0, children)
    def _(j):
        drain(j).wait()


def product(tile_rows, hi, lo, lfull, lown):
    children, listed, depth, out_width = lfull.shape
    vmem = pl.BlockSpec(memory_space=pltpu.VMEM)
    hbm = pl.BlockSpec(memory_space=pltpu.HBM)
    return pl.pallas_call(
        product_kernel,
        in_specs=[pl.BlockSpec(memory_space=pltpu.SMEM), vmem, vmem, vmem, hbm],
        out_specs=[hbm, vmem],
        out_shape=[
            jax.ShapeDtypeStruct(lown.shape, F32),
            jax.ShapeDtypeStruct((children, out_width), F32),
        ],
        scratch_shapes=[
            pltpu.VMEM(lfull.shape, F32),
            pltpu.VMEM(lown.shape, F32),
            pltpu.SemaphoreType.DMA((children,)),
            pltpu.SemaphoreType.DMA((children,)),
        ],
        compiler_params=pltpu.CompilerParams(vmem_limit_bytes=46 << 20),
        name="product",
    )(tile_rows, hi, lo, lown, lfull)


LEAF = {"z": 8, "x": 4}
COL = {"y": 8, "core": 2}


def exchange(value, axis):
    return lax.all_to_all(value, axis, split_axis=0, concat_axis=0, tiled=True)


def spread(value, axis, size):
    return exchange(jnp.broadcast_to(value[None], (size,) + value.shape), axis)


def body(root_inverse, panel, diag_inverse, tile_rows):
    local_rows, tile_count, class_width = root_inverse.shape
    tile_width = panel.shape[3]
    width = tile_count * class_width
    z, x = LEAF["z"], LEAF["x"]
    col = tuple(COL)
    col_count = COL["y"] * COL["core"]
    col_index = lax.axis_index(col)
    lhat, squares = scale(panel, diag_inverse)
    lfull = lax.all_gather(lhat, col, axis=2, tiled=True)
    root_late, _ = lax.optimization_barrier((root_inverse, lhat))
    band_rows = x * local_rows
    flat = root_late.reshape(local_rows, width)
    band = spread(flat, "x", x).reshape(band_rows, width).T.reshape(tile_count, class_width, band_rows)
    share = tile_count // x
    mine = lax.dynamic_slice_in_dim(band, lax.axis_index("x") * share, share, 0)
    quarter = lax.all_gather(mine, col, axis=1, tiled=True)
    partial = jnp.einsum(
        "ur,kr->uk",
        band.reshape(width, band_rows),
        quarter.reshape(share * tile_width, band_rows),
        precision=lax.Precision.HIGHEST,
        preferred_element_type=F32,
    )
    piece = jnp.sum(exchange(partial.reshape(z, width // z, share * tile_width), "z"), axis=0)
    sig = spread(spread(piece, "z", z), "x", x).reshape(x, width, share * tile_width)
    hi, lo, diag = prepare(col_index.reshape(1), sig, tile_count, tile_width)
    root_variance = lax.dynamic_slice_in_dim(diag, col_index * class_width, class_width, 1)
    covariance, terms = product(tile_rows, hi, lo, lfull, lhat)
    variance = squares - jnp.sum(spread(terms, col, col_count), axis=0)
    return root_variance, covariance, variance


def solution(mesh):
    sizes = {**LEAF, **COL}
    fine = Mesh(mesh.devices.reshape(tuple(sizes.values())), tuple(sizes))
    leaf, col = tuple(LEAF), tuple(COL)
    in_specs = (P(leaf, None, col), P(leaf, None, col, None), P(leaf, None, None), P(leaf, None))
    out_specs = (P(None, col), P(leaf, None, col, None), P(leaf, None))
    return jax.shard_map(body, mesh=fine, in_specs=in_specs, out_specs=out_specs, check_vma=False)
```

```python
import jax
import jax.numpy as jnp
from jax import lax
from jax.experimental import pallas as pl
from jax.experimental.pallas import tpu as pltpu
from jax.sharding import Mesh
from jax.sharding import PartitionSpec as P

F32 = jnp.float32
BF16 = jnp.bfloat16
SCALE_STEP = 3
PRODUCT_STEP = 1


def split(x):
    hi = x.astype(BF16)
    lo = (x - hi.astype(F32)).astype(BF16)
    return hi, lo


def mm(a, b):
    return jnp.dot(a, b, preferred_element_type=F32)


def put_row(ref, j, row):
    count, half = ref.shape[0] // 2, ref.shape[1]
    ref[pl.ds(j, 1), :] = row[:, :half]
    ref[pl.ds(j + count, 1), :] = row[:, half:]


def scale_kernel(panel_hbm, inverse_hbm, root_hbm, lhat_hbm, square_ref, flat_hbm, panel_buf, inverse_buf, root_buf, lhat_buf, flat_buf, panel_sem, inverse_sem, out_sem, root_sem, flat_sem):
    children = inverse_buf.shape[0]
    rows = panel_buf.shape[1] * panel_buf.shape[2]
    peers = flat_hbm.shape[0]

    def fetch(j):
        return (
            pltpu.make_async_copy(panel_hbm.at[j], panel_buf.at[j], panel_sem.at[j]),
            pltpu.make_async_copy(inverse_hbm.at[j], inverse_buf.at[j], inverse_sem.at[j]),
        )

    def drain(j):
        return pltpu.make_async_copy(lhat_buf.at[j], lhat_hbm.at[j], out_sem.at[j])

    def give(i):
        return pltpu.make_async_copy(flat_buf, flat_hbm.at[i], flat_sem.at[i])

    root_copy = pltpu.make_async_copy(root_hbm, root_buf, root_sem.at[0])
    root_copy.start()

    @pl.loop(0, children)
    def _(j):
        for copy in fetch(j):
            copy.start()

    root_copy.wait()
    flat_buf[...] = root_buf[...].reshape(-1, root_buf.shape[2]).T
    for i in range(peers):
        give(i).start()

    def one(j):
        inverse = inverse_buf[j]
        ihi, ilo = split(inverse)
        phi, plo = split(panel_buf[j].reshape(rows, inverse.shape[0]))
        both = mm(jnp.concatenate([phi, plo], axis=0), ihi)
        lhat = both[:rows] + (both[rows:] + mm(phi, ilo))
        lhat_buf[j] = lhat.reshape(lhat_buf.shape[1:])
        put_row(square_ref, j, jnp.sum(inverse * inverse, axis=0, keepdims=True))

    @pl.loop(0, children // SCALE_STEP)
    def _(i):
        group = [i * SCALE_STEP + u for u in range(SCALE_STEP)]
        for j in group:
            for copy in fetch(j):
                copy.wait()
        for j in group:
            one(j)
        for j in group:
            drain(j).start()

    @pl.loop(0, children)
    def _(j):
        drain(j).wait()

    for i in range(peers):
        give(i).wait()


def scale(panel, inverse, root, peers):
    children, _, wide = inverse.shape
    flat = (root.shape[2], root.shape[0] * root.shape[1])
    hbm = pl.BlockSpec(memory_space=pltpu.HBM)
    return pl.pallas_call(
        scale_kernel,
        in_specs=[hbm, hbm, hbm],
        out_specs=[hbm, pl.BlockSpec(memory_space=pltpu.VMEM), hbm],
        out_shape=[
            jax.ShapeDtypeStruct(panel.shape, F32),
            jax.ShapeDtypeStruct((2 * children, wide // 2), F32),
            jax.ShapeDtypeStruct((peers,) + flat, F32),
        ],
        scratch_shapes=[
            pltpu.VMEM(panel.shape, F32),
            pltpu.VMEM(inverse.shape, F32),
            pltpu.VMEM(root.shape, F32),
            pltpu.VMEM(panel.shape, F32),
            pltpu.VMEM(flat, F32),
            pltpu.SemaphoreType.DMA((children,)),
            pltpu.SemaphoreType.DMA((children,)),
            pltpu.SemaphoreType.DMA((children,)),
            pltpu.SemaphoreType.DMA((1,)),
            pltpu.SemaphoreType.DMA((peers,)),
        ],
        name="scale",
    )(panel, inverse, root)


def product_kernel(rows_ref, col_ref, sig_ref, lfull_hbm, cov_hbm, term_ref, diag_ref, hi_ref, lo_ref, lfull_buf, cov_buf, sum_ref, in_sem, out_sem):
    children, listed, depth, out_width = lfull_buf.shape
    tiles, width, _ = hi_ref.shape
    cls = width // tiles

    def fetch(j):
        return pltpu.make_async_copy(lfull_hbm.at[j], lfull_buf.at[j], in_sem.at[j])

    def drain(j):
        return pltpu.make_async_copy(cov_buf.at[j], cov_hbm.at[j], out_sem.at[j])

    @pl.loop(0, children)
    def _(j):
        fetch(j).start()

    share = sig_ref.shape[2] // depth
    first = col_ref[0] * cls
    lane = lax.broadcasted_iota(jnp.int32, (cls, depth), 1)
    row = lax.broadcasted_iota(jnp.int32, (cls, depth), 0)
    on_diag = lane == row + first
    for p in range(tiles):
        part, place = divmod(p, share)
        block = sig_ref[part, :, place * depth : (place + 1) * depth]
        hi, lo = split(block)
        hi_ref[p] = hi
        lo_ref[p] = lo
        own = block[p * cls : (p + 1) * cls]
        diag_ref[p : p + 1, :] = jnp.sum(jnp.where(on_diag, own, 0.0), axis=0, keepdims=True)

    def one(j):
        picks = [pl.ds(pl.multiple_of(rows_ref[j, q] * cls, cls), cls) for q in range(listed)]
        rows = listed * cls
        acc = None
        for p in range(listed):
            tp = rows_ref[j, p]
            both = jnp.concatenate([hi_ref[tp, s, :] for s in picks] + [lo_ref[tp, s, :] for s in picks], axis=0)
            lhi, llo = split(lfull_buf[j, p])
            lead = mm(both, lhi)
            term = lead[:rows] + (lead[rows:] + mm(both[:rows], llo))
            acc = term if acc is None else acc + term
        cov = -acc
        cov_buf[j] = cov.reshape(cov_buf.shape[1:])
        own = lfull_buf[j, :, pl.ds(pl.multiple_of(first, cls), cls), :].reshape(cov.shape)
        put_row(sum_ref, j, jnp.sum(own * cov, axis=0, keepdims=True))

    @pl.loop(0, children // PRODUCT_STEP)
    def _(i):
        group = [i * PRODUCT_STEP + u for u in range(PRODUCT_STEP)]
        for j in group:
            fetch(j).wait()
        for j in group:
            one(j)
        for j in group:
            drain(j).start()

    sums = sum_ref[...]
    for i in range(term_ref.shape[0]):
        term_ref[i] = sums

    @pl.loop(0, children)
    def _(j):
        drain(j).wait()


def product(tile_rows, col, sig, lfull, peers):
    children, listed, depth, out_width = lfull.shape
    width = sig.shape[1]
    tiles = sig.shape[0] * sig.shape[2] // depth
    lines = (2 * children, out_width // 2)
    strips = (children, listed, width // tiles, out_width)
    vmem = pl.BlockSpec(memory_space=pltpu.VMEM)
    smem = pl.BlockSpec(memory_space=pltpu.SMEM)
    hbm = pl.BlockSpec(memory_space=pltpu.HBM)
    return pl.pallas_call(
        product_kernel,
        in_specs=[smem, smem, vmem, hbm],
        out_specs=[hbm, vmem, vmem],
        out_shape=[
            jax.ShapeDtypeStruct(strips, F32),
            jax.ShapeDtypeStruct((peers,) + lines, F32),
            jax.ShapeDtypeStruct((tiles, depth), F32),
        ],
        scratch_shapes=[
            pltpu.VMEM((tiles, width, depth), BF16),
            pltpu.VMEM((tiles, width, depth), BF16),
            pltpu.VMEM(lfull.shape, F32),
            pltpu.VMEM(strips, F32),
            pltpu.VMEM(lines, F32),
            pltpu.SemaphoreType.DMA((children,)),
            pltpu.SemaphoreType.DMA((children,)),
        ],
        compiler_params=pltpu.CompilerParams(vmem_limit_bytes=46 << 20),
        name="product",
    )(tile_rows, col, sig, lfull)


LEAF = {"z": 8, "x": 4}
COL = {"y": 8, "core": 2}


def exchange(value, axis):
    return lax.all_to_all(value, axis, split_axis=0, concat_axis=0, tiled=True)


def spread(value, axis, size):
    return exchange(jnp.broadcast_to(value[None], (size,) + value.shape), axis)


def body(root_inverse, panel, diag_inverse, tile_rows):
    local_rows, tile_count, class_width = root_inverse.shape
    tile_width = panel.shape[3]
    width = tile_count * class_width
    z, x = LEAF["z"], LEAF["x"]
    col = tuple(COL)
    col_count = COL["y"] * COL["core"]
    col_index = lax.axis_index(col)
    lhat, squares, flat = scale(panel, diag_inverse, root_inverse.transpose(1, 2, 0), x)
    lfull = lax.all_gather(lhat, col, axis=2, tiled=True)
    band_rows = x * local_rows
    band = exchange(flat, "x").reshape(band_rows, width).T.reshape(tile_count, class_width, band_rows)
    share = tile_count // x
    mine = lax.dynamic_slice_in_dim(band, lax.axis_index("x") * share, share, 0)
    quarter = lax.all_gather(mine, col, axis=1, tiled=True)
    partial = jnp.einsum(
        "ur,kr->uk",
        band.reshape(width, band_rows),
        quarter.reshape(share * tile_width, band_rows),
        precision=lax.Precision.HIGHEST,
        preferred_element_type=F32,
    )
    piece = jnp.sum(exchange(partial.reshape(z, width // z, share * tile_width), "z"), axis=0)
    sig = spread(spread(piece, "z", z), "x", x).reshape(x, width, share * tile_width)
    covariance, terms, diag = product(tile_rows, col_index.reshape(1), sig, lfull, col_count)
    root_variance = lax.dynamic_slice_in_dim(diag, col_index * class_width, class_width, 1)
    halves = squares - jnp.sum(exchange(terms, col), axis=0)
    count = diag_inverse.shape[0]
    variance = jnp.concatenate([halves[:count], halves[count:]], axis=1)
    return root_variance, covariance, variance


def solution(mesh):
    sizes = {**LEAF, **COL}
    fine = Mesh(mesh.devices.reshape(tuple(sizes.values())), tuple(sizes))
    leaf, col = tuple(LEAF), tuple(COL)
    in_specs = (P(leaf, None, col), P(leaf, None, col, None), P(leaf, None, None), P(leaf, None))
    out_specs = (P(None, col), P(leaf, None, col, None), P(leaf, None))
    return jax.shard_map(body, mesh=fine, in_specs=in_specs, out_specs=out_specs, check_vma=False)
```

```python
import jax
import jax.numpy as jnp
from jax import lax
from jax.experimental import pallas as pl
from jax.experimental.pallas import tpu as pltpu
from jax.sharding import Mesh
from jax.sharding import PartitionSpec as P

F32 = jnp.float32
BF16 = jnp.bfloat16
SCALE_STEP = 3
PRODUCT_STEP = 1
LEAF = {"z": 8, "x": 4}
COL = {"y": 8, "core": 2}


def split(x):
    hi = x.astype(BF16)
    lo = (x - hi.astype(F32)).astype(BF16)
    return hi, lo


def mm(a, b):
    return jnp.dot(a, b, preferred_element_type=F32)


def put_row(ref, j, row):
    count, half = ref.shape[0] // 2, ref.shape[1]
    ref[pl.ds(j, 1), :] = row[:, :half]
    ref[pl.ds(j + count, 1), :] = row[:, half:]


def scale_kernel(panel_hbm, inverse_hbm, root_hbm, lhat_hbm, square_ref, flat_hbm, panel_buf, inverse_buf, root_buf, lhat_buf, flat_buf, panel_sem, inverse_sem, out_sem, root_sem, flat_sem):
    children = inverse_buf.shape[0]
    rows = panel_buf.shape[1] * panel_buf.shape[2]
    peers = flat_hbm.shape[0]

    def fetch(j):
        return (
            pltpu.make_async_copy(panel_hbm.at[j], panel_buf.at[j], panel_sem.at[j]),
            pltpu.make_async_copy(inverse_hbm.at[j], inverse_buf.at[j], inverse_sem.at[j]),
        )

    def drain(j):
        return pltpu.make_async_copy(lhat_buf.at[j], lhat_hbm.at[j], out_sem.at[j])

    def give(i):
        return pltpu.make_async_copy(flat_buf, flat_hbm.at[i], flat_sem.at[i])

    root_copy = pltpu.make_async_copy(root_hbm, root_buf, root_sem.at[0])
    root_copy.start()

    @pl.loop(0, children)
    def _(j):
        for copy in fetch(j):
            copy.start()

    root_copy.wait()
    flat_buf[...] = root_buf[...].reshape(-1, root_buf.shape[2]).T
    for i in range(peers):
        give(i).start()

    def one(j):
        inverse = inverse_buf[j]
        ihi, ilo = split(inverse)
        phi, plo = split(panel_buf[j].reshape(rows, inverse.shape[0]))
        both = mm(jnp.concatenate([phi, plo], axis=0), ihi)
        lhat = both[:rows] + (both[rows:] + mm(phi, ilo))
        lhat_buf[j] = lhat.reshape(lhat_buf.shape[1:])
        put_row(square_ref, j, jnp.sum(inverse * inverse, axis=0, keepdims=True))

    @pl.loop(0, children // SCALE_STEP)
    def _(i):
        group = [i * SCALE_STEP + u for u in range(SCALE_STEP)]
        for j in group:
            for copy in fetch(j):
                copy.wait()
        for j in group:
            one(j)
        for j in group:
            drain(j).start()

    @pl.loop(0, children)
    def _(j):
        drain(j).wait()

    for i in range(peers):
        give(i).wait()


def scale(panel, inverse, root, peers):
    children, _, wide = inverse.shape
    flat = (root.shape[2], root.shape[0] * root.shape[1])
    hbm = pl.BlockSpec(memory_space=pltpu.HBM)
    return pl.pallas_call(
        scale_kernel,
        in_specs=[hbm, hbm, hbm],
        out_specs=[hbm, pl.BlockSpec(memory_space=pltpu.VMEM), hbm],
        out_shape=[
            jax.ShapeDtypeStruct(panel.shape, F32),
            jax.ShapeDtypeStruct((2 * children, wide // 2), F32),
            jax.ShapeDtypeStruct((peers,) + flat, F32),
        ],
        scratch_shapes=[
            pltpu.VMEM(panel.shape, F32),
            pltpu.VMEM(inverse.shape, F32),
            pltpu.VMEM(root.shape, F32),
            pltpu.VMEM(panel.shape, F32),
            pltpu.VMEM(flat, F32),
            pltpu.SemaphoreType.DMA((children,)),
            pltpu.SemaphoreType.DMA((children,)),
            pltpu.SemaphoreType.DMA((children,)),
            pltpu.SemaphoreType.DMA((1,)),
            pltpu.SemaphoreType.DMA((peers,)),
        ],
        name="scale",
    )(panel, inverse, root)


def product_kernel(rows_ref, sig_ref, square_ref, lfull_hbm, cov_hbm, term_ref, root_ref, diag_ref, hi_ref, lo_ref, lfull_buf, cov_buf, sum_ref, in_sem, out_sem):
    children, listed, depth, out_width = lfull_buf.shape
    tiles, width, _ = hi_ref.shape
    cls = width // tiles

    def fetch(j):
        return pltpu.make_async_copy(lfull_hbm.at[j], lfull_buf.at[j], in_sem.at[j])

    def drain(j):
        return pltpu.make_async_copy(cov_buf.at[j], cov_hbm.at[j], out_sem.at[j])

    @pl.loop(0, children)
    def _(j):
        fetch(j).start()

    share = sig_ref.shape[2] // depth
    col = lax.axis_index("y") * COL["core"] + lax.axis_index("core")
    first = col * cls
    lane = lax.broadcasted_iota(jnp.int32, (cls, depth), 1)
    row = lax.broadcasted_iota(jnp.int32, (cls, depth), 0)
    on_diag = lane == row + first
    for p in range(tiles):
        part, place = divmod(p, share)
        block = sig_ref[part, :, place * depth : (place + 1) * depth]
        hi, lo = split(block)
        hi_ref[p] = hi
        lo_ref[p] = lo
        own = block[p * cls : (p + 1) * cls]
        diag_ref[p : p + 1, :] = jnp.sum(jnp.where(on_diag, own, 0.0), axis=0, keepdims=True)

    root_ref[...] = pltpu.roll(diag_ref[...], lax.rem(depth - first, depth), 1)[:, :cls]

    def one(j):
        picks = [pl.ds(pl.multiple_of(rows_ref[q, j] * cls, cls), cls) for q in range(listed)]
        rows = listed * cls
        acc = None
        for p in range(listed):
            tp = rows_ref[p, j]
            both = jnp.concatenate([hi_ref[tp, s, :] for s in picks] + [lo_ref[tp, s, :] for s in picks], axis=0)
            lhi, llo = split(lfull_buf[j, p])
            lead = mm(both, lhi)
            term = lead[:rows] + (lead[rows:] + mm(both[:rows], llo))
            acc = term if acc is None else acc + term
        cov = -acc
        cov_buf[j] = cov.reshape(cov_buf.shape[1:])
        own = lfull_buf[j, :, pl.ds(pl.multiple_of(first, cls), cls), :].reshape(cov.shape)
        put_row(sum_ref, j, jnp.sum(own * cov, axis=0, keepdims=True))

    @pl.loop(0, children // PRODUCT_STEP)
    def _(i):
        group = [i * PRODUCT_STEP + u for u in range(PRODUCT_STEP)]
        for j in group:
            fetch(j).wait()
        for j in group:
            one(j)
        for j in group:
            drain(j).start()

    sums = jnp.where(col == 0, square_ref[...], 0.0) - sum_ref[...]
    for i in range(term_ref.shape[0]):
        term_ref[i] = sums

    @pl.loop(0, children)
    def _(j):
        drain(j).wait()


def product(tile_rows, sig, squares, lfull, peers):
    children, listed, depth, out_width = lfull.shape
    width = sig.shape[1]
    tiles = sig.shape[0] * sig.shape[2] // depth
    lines = (2 * children, out_width // 2)
    strips = (children, listed, width // tiles, out_width)
    vmem = pl.BlockSpec(memory_space=pltpu.VMEM)
    smem = pl.BlockSpec(memory_space=pltpu.SMEM)
    hbm = pl.BlockSpec(memory_space=pltpu.HBM)
    return pl.pallas_call(
        product_kernel,
        in_specs=[smem, vmem, vmem, hbm],
        out_specs=[hbm, vmem, vmem],
        out_shape=[
            jax.ShapeDtypeStruct(strips, F32),
            jax.ShapeDtypeStruct((peers,) + lines, F32),
            jax.ShapeDtypeStruct((tiles, width // tiles), F32),
        ],
        scratch_shapes=[
            pltpu.VMEM((tiles, depth), F32),
            pltpu.VMEM((tiles, width, depth), BF16),
            pltpu.VMEM((tiles, width, depth), BF16),
            pltpu.VMEM(lfull.shape, F32),
            pltpu.VMEM(strips, F32),
            pltpu.VMEM(lines, F32),
            pltpu.SemaphoreType.DMA((children,)),
            pltpu.SemaphoreType.DMA((children,)),
        ],
        compiler_params=pltpu.CompilerParams(vmem_limit_bytes=46 << 20),
        name="product",
    )(tile_rows, sig, squares, lfull)


def exchange(value, axis):
    return lax.all_to_all(value, axis, split_axis=0, concat_axis=0, tiled=True)


def spread(value, axis, size):
    return exchange(jnp.broadcast_to(value[None], (size,) + value.shape), axis)


def body(root_inverse, panel, diag_inverse, tile_rows):
    local_rows, tile_count, class_width = root_inverse.shape
    tile_width = panel.shape[3]
    width = tile_count * class_width
    z, x = LEAF["z"], LEAF["x"]
    col = tuple(COL)
    col_count = COL["y"] * COL["core"]
    lhat, squares, flat = scale(panel, diag_inverse, root_inverse.transpose(1, 2, 0), x)
    lfull = lax.all_gather(lhat, col, axis=2, tiled=True)
    band_rows = x * local_rows
    share = tile_count // x
    flat, start = lax.optimization_barrier((flat, lax.axis_index("x") * share))
    band = exchange(flat, "x").reshape(band_rows, width).T.reshape(tile_count, class_width, band_rows)
    mine = lax.dynamic_slice_in_dim(band, start, share, 0)
    quarter = lax.all_gather(mine, col, axis=1, tiled=True)
    partial = jnp.einsum(
        "ur,kr->uk",
        band.reshape(width, band_rows),
        quarter.reshape(share * tile_width, band_rows),
        precision=lax.Precision.HIGHEST,
        preferred_element_type=F32,
    )
    piece = jnp.sum(exchange(partial.reshape(z, width // z, share * tile_width), "z"), axis=0)
    sig = spread(spread(piece, "z", z), "x", x).reshape(x, width, share * tile_width)
    covariance, terms, root_variance = product(tile_rows.T, sig, squares, lfull, col_count)
    halves = jnp.sum(exchange(terms, col), axis=0)
    count = diag_inverse.shape[0]
    variance = jnp.concatenate([halves[:count], halves[count:]], axis=1)
    return root_variance, covariance, variance


def solution(mesh):
    sizes = {**LEAF, **COL}
    fine = Mesh(mesh.devices.reshape(tuple(sizes.values())), tuple(sizes))
    leaf, col = tuple(LEAF), tuple(COL)
    in_specs = (P(leaf, None, col), P(leaf, None, col, None), P(leaf, None, None), P(leaf, None))
    out_specs = (P(None, col), P(leaf, None, col, None), P(leaf, None))
    return jax.shard_map(body, mesh=fine, in_specs=in_specs, out_specs=out_specs, check_vma=False)
```

```python
import jax
import jax.numpy as jnp
from jax import lax
from jax.experimental import pallas as pl
from jax.experimental.pallas import tpu as pltpu
from jax.sharding import Mesh
from jax.sharding import PartitionSpec as P

F32 = jnp.float32
BF16 = jnp.bfloat16
SCALE_STEP = 4
PRODUCT_STEP = 1
LEAF = {"z": 8, "x": 4}
COL = {"y": 8, "core": 2}


def split(x):
    hi = x.astype(BF16)
    lo = (x - hi.astype(F32)).astype(BF16)
    return hi, lo


def mm(a, b):
    return jnp.dot(a, b, preferred_element_type=F32)


def put_row(ref, j, row):
    count, half = ref.shape[0] // 2, ref.shape[1]
    ref[pl.ds(j, 1), :] = row[:, :half]
    ref[pl.ds(j + count, 1), :] = row[:, half:]


def scale_kernel(panel_hbm, inverse_hbm, root_hbm, lhat_hbm, square_ref, flat_hbm, panel_buf, inverse_buf, root_buf, lhat_buf, flat_buf, panel_sem, out_sem, root_sem, flat_sem):
    children = inverse_buf.shape[0]
    rows = panel_buf.shape[1] * panel_buf.shape[2]
    peers = flat_hbm.shape[0]

    half = inverse_buf.shape[1] // 2
    top, low, left = pl.ds(0, half), pl.ds(half, half), pl.ds(0, half)

    groups = children // SCALE_STEP

    def some(i):
        return pl.ds(i * SCALE_STEP, SCALE_STEP)

    def fetch(i):
        return (
            pltpu.make_async_copy(panel_hbm.at[some(i)], panel_buf.at[some(i)], panel_sem.at[0, i]),
            pltpu.make_async_copy(inverse_hbm.at[some(i), top, left], inverse_buf.at[some(i), top, left], panel_sem.at[1, i]),
            pltpu.make_async_copy(inverse_hbm.at[some(i), low, :], inverse_buf.at[some(i), low, :], panel_sem.at[2, i]),
        )

    def drain(i):
        return pltpu.make_async_copy(lhat_buf.at[some(i)], lhat_hbm.at[some(i)], out_sem.at[i])

    def give(i):
        return pltpu.make_async_copy(flat_buf, flat_hbm.at[i], flat_sem.at[i])

    root_copy = pltpu.make_async_copy(root_hbm, root_buf, root_sem.at[0])
    for i in range(groups):
        for copy in fetch(i):
            copy.start()
        if i == 0:
            root_copy.start()

    root_copy.wait()
    flat_buf[...] = root_buf[...].reshape(-1, root_buf.shape[2]).T
    for i in range(peers):
        give(i).start()

    def one(j):
        first, second = inverse_buf[j, top, left], inverse_buf[j, low, :]
        fhi, flo = split(first)
        shi, slo = split(second)
        phi, plo = split(panel_buf[j].reshape(rows, 2 * half))
        pair = jnp.concatenate([phi, plo], axis=0)
        upper = mm(pair[:, :half], fhi)
        lower = mm(pair[:, half:], shi)
        upper = upper[:rows] + (upper[rows:] + mm(phi[:, :half], flo))
        lower = lower[:rows] + (lower[rows:] + mm(phi[:, half:], slo))
        lhat = jnp.concatenate([lower[:, :half] + upper, lower[:, half:]], axis=1)
        lhat_buf[j] = lhat.reshape(lhat_buf.shape[1:])
        squares = jnp.sum(second * second, axis=0, keepdims=True)
        before = jnp.sum(first * first, axis=0, keepdims=True)
        put_row(square_ref, j, jnp.concatenate([squares[:, :half] + before, squares[:, half:]], axis=1))

    @pl.loop(0, groups)
    def _(i):
        for copy in fetch(i):
            copy.wait()
        for u in range(SCALE_STEP):
            one(i * SCALE_STEP + u)
        drain(i).start()

    for i in range(groups):
        drain(i).wait()
    for i in range(peers):
        give(i).wait()


def scale(panel, inverse, root, peers):
    children, _, wide = inverse.shape
    flat = (root.shape[2], root.shape[0] * root.shape[1])
    hbm = pl.BlockSpec(memory_space=pltpu.HBM)
    return pl.pallas_call(
        scale_kernel,
        in_specs=[hbm, hbm, hbm],
        out_specs=[hbm, pl.BlockSpec(memory_space=pltpu.VMEM), hbm],
        out_shape=[
            jax.ShapeDtypeStruct(panel.shape, F32),
            jax.ShapeDtypeStruct((2 * children, wide // 2), F32),
            jax.ShapeDtypeStruct((peers,) + flat, F32),
        ],
        scratch_shapes=[
            pltpu.VMEM(panel.shape, F32),
            pltpu.VMEM(inverse.shape, F32),
            pltpu.VMEM(root.shape, F32),
            pltpu.VMEM(panel.shape, F32),
            pltpu.VMEM(flat, F32),
            pltpu.SemaphoreType.DMA((3, children // SCALE_STEP)),
            pltpu.SemaphoreType.DMA((children // SCALE_STEP,)),
            pltpu.SemaphoreType.DMA((1,)),
            pltpu.SemaphoreType.DMA((peers,)),
        ],
        name="scale",
    )(panel, inverse, root)


def product_kernel(rows_ref, sig_ref, square_ref, lfull_hbm, cov_hbm, term_ref, root_ref, diag_ref, hi_ref, lo_ref, lfull_buf, cov_buf, sum_ref, in_sem, out_sem):
    children, listed, depth, out_width = lfull_buf.shape
    tiles, width, _ = hi_ref.shape
    cls = width // tiles

    def fetch(j):
        return pltpu.make_async_copy(lfull_hbm.at[j], lfull_buf.at[j], in_sem.at[j])

    def drain(j):
        return pltpu.make_async_copy(cov_buf.at[j], cov_hbm.at[j], out_sem.at[j])

    @pl.loop(0, children)
    def _(j):
        fetch(j).start()

    share = sig_ref.shape[2] // depth
    col = lax.axis_index("y") * COL["core"] + lax.axis_index("core")
    first = col * cls
    lane = lax.broadcasted_iota(jnp.int32, (cls, depth), 1)
    row = lax.broadcasted_iota(jnp.int32, (cls, depth), 0)
    on_diag = lane == row + first
    for p in range(tiles):
        part, place = divmod(p, share)
        block = sig_ref[part, :, place * depth : (place + 1) * depth]
        hi, lo = split(block)
        hi_ref[p] = hi
        lo_ref[p] = lo
        own = block[p * cls : (p + 1) * cls]
        diag_ref[p : p + 1, :] = jnp.sum(jnp.where(on_diag, own, 0.0), axis=0, keepdims=True)

    root_ref[...] = pltpu.roll(diag_ref[...], lax.rem(depth - first, depth), 1)[:, :cls]

    def one(j):
        picks = [pl.ds(pl.multiple_of(rows_ref[q, j], cls), cls) for q in range(listed)]
        rows = listed * cls
        acc = None
        for p in range(listed):
            tp = rows_ref[p, j] // cls
            both = jnp.concatenate([hi_ref[tp, s, :] for s in picks] + [lo_ref[tp, s, :] for s in picks], axis=0)
            lhi, llo = split(lfull_buf[j, p])
            lead = mm(both, lhi)
            term = lead[:rows] + (lead[rows:] + mm(both[:rows], llo))
            acc = term if acc is None else acc + term
        cov = -acc
        cov_buf[j] = cov.reshape(cov_buf.shape[1:])
        own = lfull_buf[j, :, pl.ds(pl.multiple_of(first, cls), cls), :].reshape(cov.shape)
        put_row(sum_ref, j, jnp.sum(own * cov, axis=0, keepdims=True))

    @pl.loop(0, children // PRODUCT_STEP)
    def _(i):
        group = [i * PRODUCT_STEP + u for u in range(PRODUCT_STEP)]
        for j in group:
            fetch(j).wait()
        for j in group:
            one(j)
        for j in group:
            drain(j).start()

    sums = square_ref[...] - sum_ref[...]
    for i in range(term_ref.shape[0]):
        term_ref[i] = sums

    @pl.loop(0, children)
    def _(j):
        drain(j).wait()


def product(tile_rows, sig, squares, lfull, peers):
    children, listed, depth, out_width = lfull.shape
    width = sig.shape[1]
    tiles = sig.shape[0] * sig.shape[2] // depth
    lines = (2 * children, out_width // 2)
    strips = (children, listed, width // tiles, out_width)
    vmem = pl.BlockSpec(memory_space=pltpu.VMEM)
    smem = pl.BlockSpec(memory_space=pltpu.SMEM)
    hbm = pl.BlockSpec(memory_space=pltpu.HBM)
    return pl.pallas_call(
        product_kernel,
        in_specs=[smem, vmem, vmem, hbm],
        out_specs=[hbm, vmem, vmem],
        out_shape=[
            jax.ShapeDtypeStruct(strips, F32),
            jax.ShapeDtypeStruct((peers,) + lines, F32),
            jax.ShapeDtypeStruct((tiles, width // tiles), F32),
        ],
        scratch_shapes=[
            pltpu.VMEM((tiles, depth), F32),
            pltpu.VMEM((tiles, width, depth), BF16),
            pltpu.VMEM((tiles, width, depth), BF16),
            pltpu.VMEM(lfull.shape, F32),
            pltpu.VMEM(strips, F32),
            pltpu.VMEM(lines, F32),
            pltpu.SemaphoreType.DMA((children,)),
            pltpu.SemaphoreType.DMA((children,)),
        ],
        compiler_params=pltpu.CompilerParams(vmem_limit_bytes=46 << 20),
        name="product",
    )(tile_rows, sig, squares, lfull)


def exchange(value, axis):
    return lax.all_to_all(value, axis, split_axis=0, concat_axis=0, tiled=True)


def spread(value, axis, size):
    return exchange(jnp.broadcast_to(value[None], (size,) + value.shape), axis)


def body(root_inverse, panel, diag_inverse, tile_rows):
    local_rows, tile_count, class_width = root_inverse.shape
    tile_width = panel.shape[3]
    width = tile_count * class_width
    z, x = LEAF["z"], LEAF["x"]
    col = tuple(COL)
    col_count = COL["y"] * COL["core"]
    lhat, squares, flat = scale(panel, diag_inverse, root_inverse.transpose(1, 2, 0), x)
    lfull = lax.all_gather(lhat, col, axis=2, tiled=True)
    band_rows = x * local_rows
    share = tile_count // x
    flat, start = lax.optimization_barrier((flat, lax.axis_index("x") * share))
    bands = exchange(flat, "x")
    squares = jnp.where(lax.axis_index(col) == 0, squares, 0.0)
    bands, squares, picked = lax.optimization_barrier((bands, squares, tile_rows.T * class_width))
    band = bands.reshape(band_rows, width).T.reshape(tile_count, class_width, band_rows)
    mine = lax.dynamic_slice_in_dim(band, start, share, 0)
    quarter = lax.all_gather(mine, col, axis=1, tiled=True)
    partial = jnp.einsum(
        "ur,kr->uk",
        band.reshape(width, band_rows),
        quarter.reshape(share * tile_width, band_rows),
        precision=lax.Precision.HIGHEST,
        preferred_element_type=F32,
    )
    piece = jnp.sum(exchange(partial.reshape(z, width // z, share * tile_width), "z"), axis=0)
    sig = spread(spread(piece, "z", z), "x", x).reshape(x, width, share * tile_width)
    covariance, terms, root_variance = product(picked, sig, squares, lfull, col_count)
    halves = jnp.sum(exchange(terms, col), axis=0)
    count = diag_inverse.shape[0]
    variance = jnp.concatenate([halves[:count], halves[count:]], axis=1)
    return root_variance, covariance, variance


def solution(mesh):
    sizes = {**LEAF, **COL}
    fine = Mesh(mesh.devices.reshape(tuple(sizes.values())), tuple(sizes))
    leaf, col = tuple(LEAF), tuple(COL)
    in_specs = (P(leaf, None, col), P(leaf, None, col, None), P(leaf, None, None), P(leaf, None))
    out_specs = (P(None, col), P(leaf, None, col, None), P(leaf, None))
    return jax.shard_map(body, mesh=fine, in_specs=in_specs, out_specs=out_specs, check_vma=False)
```

```python
import jax
import jax.numpy as jnp
from jax import lax
from jax.experimental import pallas as pl
from jax.experimental.pallas import tpu as pltpu
from jax.sharding import Mesh
from jax.sharding import PartitionSpec as P

F32 = jnp.float32
BF16 = jnp.bfloat16
SCALE_STEP = 4
PRODUCT_STEP = 1
LEAF = {"far": 4, "near": 2, "x": 4}
COL = {"y": 8, "core": 2}


def split(x):
    hi = x.astype(BF16)
    lo = (x - hi.astype(F32)).astype(BF16)
    return hi, lo


def mm(a, b):
    return jnp.dot(a, b, preferred_element_type=F32)


def put_row(ref, j, row):
    count, half = ref.shape[0] // 2, ref.shape[1]
    ref[pl.ds(j, 1), :] = row[:, :half]
    ref[pl.ds(j + count, 1), :] = row[:, half:]


def scale_kernel(panel_hbm, inverse_hbm, root_hbm, lhat_hbm, square_ref, flat_hbm, panel_buf, inverse_buf, root_buf, lhat_buf, flat_buf, panel_sem, out_sem, root_sem, flat_sem):
    children = inverse_buf.shape[0]
    rows = panel_buf.shape[1] * panel_buf.shape[2]
    peers = flat_hbm.shape[0]

    half = inverse_buf.shape[1] // 2
    top, low, left = pl.ds(0, half), pl.ds(half, half), pl.ds(0, half)

    groups = children // SCALE_STEP

    def some(i):
        return pl.ds(i * SCALE_STEP, SCALE_STEP)

    def fetch(i):
        return (
            pltpu.make_async_copy(panel_hbm.at[some(i)], panel_buf.at[some(i)], panel_sem.at[0, i]),
            pltpu.make_async_copy(inverse_hbm.at[some(i), top, left], inverse_buf.at[some(i), top, left], panel_sem.at[1, i]),
            pltpu.make_async_copy(inverse_hbm.at[some(i), low, :], inverse_buf.at[some(i), low, :], panel_sem.at[2, i]),
        )

    def drain(i):
        return pltpu.make_async_copy(lhat_buf.at[some(i)], lhat_hbm.at[some(i)], out_sem.at[i])

    def give(i):
        return pltpu.make_async_copy(flat_buf, flat_hbm.at[i], flat_sem.at[i])

    root_copy = pltpu.make_async_copy(root_hbm, root_buf, root_sem.at[0])
    for i in range(groups):
        for copy in fetch(i):
            copy.start()
        if i == 0:
            root_copy.start()

    root_copy.wait()
    flat_buf[...] = root_buf[...].reshape(-1, root_buf.shape[2]).T
    for i in range(peers):
        give(i).start()

    def one(j):
        first, second = inverse_buf[j, top, left], inverse_buf[j, low, :]
        fhi, flo = split(first)
        shi, slo = split(second)
        phi, plo = split(panel_buf[j].reshape(rows, 2 * half))
        pair = jnp.concatenate([phi, plo], axis=0)
        upper = mm(pair[:, :half], fhi)
        lower = mm(pair[:, half:], shi)
        upper = upper[:rows] + (upper[rows:] + mm(phi[:, :half], flo))
        lower = lower[:rows] + (lower[rows:] + mm(phi[:, half:], slo))
        lhat = jnp.concatenate([lower[:, :half] + upper, lower[:, half:]], axis=1)
        lhat_buf[j] = lhat.reshape(lhat_buf.shape[1:])
        squares = jnp.sum(second * second, axis=0, keepdims=True)
        before = jnp.sum(first * first, axis=0, keepdims=True)
        put_row(square_ref, j, jnp.concatenate([squares[:, :half] + before, squares[:, half:]], axis=1))

    @pl.loop(0, groups)
    def _(i):
        for copy in fetch(i):
            copy.wait()
        for u in range(SCALE_STEP):
            one(i * SCALE_STEP + u)
        drain(i).start()

    for i in range(groups):
        drain(i).wait()
    for i in range(peers):
        give(i).wait()


def scale(panel, inverse, root, peers):
    children, _, wide = inverse.shape
    flat = (root.shape[2], root.shape[0] * root.shape[1])
    hbm = pl.BlockSpec(memory_space=pltpu.HBM)
    return pl.pallas_call(
        scale_kernel,
        in_specs=[hbm, hbm, hbm],
        out_specs=[hbm, pl.BlockSpec(memory_space=pltpu.VMEM), hbm],
        out_shape=[
            jax.ShapeDtypeStruct(panel.shape, F32),
            jax.ShapeDtypeStruct((2 * children, wide // 2), F32),
            jax.ShapeDtypeStruct((peers,) + flat, F32),
        ],
        scratch_shapes=[
            pltpu.VMEM(panel.shape, F32),
            pltpu.VMEM(inverse.shape, F32),
            pltpu.VMEM(root.shape, F32),
            pltpu.VMEM(panel.shape, F32),
            pltpu.VMEM(flat, F32),
            pltpu.SemaphoreType.DMA((3, children // SCALE_STEP)),
            pltpu.SemaphoreType.DMA((children // SCALE_STEP,)),
            pltpu.SemaphoreType.DMA((1,)),
            pltpu.SemaphoreType.DMA((peers,)),
        ],
        name="scale",
    )(panel, inverse, root)


def product_kernel(rows_ref, sig_ref, square_ref, lfull_hbm, cov_hbm, term_ref, root_ref, diag_ref, hi_ref, lo_ref, lfull_buf, cov_buf, sum_ref, in_sem, out_sem):
    children, listed, depth, out_width = lfull_buf.shape
    tiles, width, _ = hi_ref.shape
    cls = width // tiles

    def fetch(j):
        return pltpu.make_async_copy(lfull_hbm.at[j], lfull_buf.at[j], in_sem.at[j])

    def drain(j):
        return pltpu.make_async_copy(cov_buf.at[j], cov_hbm.at[j], out_sem.at[j])

    @pl.loop(0, children)
    def _(j):
        fetch(j).start()

    share = sig_ref.shape[2] // depth
    col = lax.axis_index("y") * COL["core"] + lax.axis_index("core")
    first = col * cls
    lane = lax.broadcasted_iota(jnp.int32, (cls, depth), 1)
    row = lax.broadcasted_iota(jnp.int32, (cls, depth), 0)
    on_diag = lane == row + first
    for p in range(tiles):
        part, place = divmod(p, share)
        block = sig_ref[part, :, place * depth : (place + 1) * depth]
        hi, lo = split(block)
        hi_ref[p] = hi
        lo_ref[p] = lo
        own = block[p * cls : (p + 1) * cls]
        diag_ref[p : p + 1, :] = jnp.sum(jnp.where(on_diag, own, 0.0), axis=0, keepdims=True)

    root_ref[...] = pltpu.roll(diag_ref[...], lax.rem(depth - first, depth), 1)[:, :cls]

    def one(j):
        picks = [pl.ds(pl.multiple_of(rows_ref[q, j], cls), cls) for q in range(listed)]
        rows = listed * cls
        acc = None
        for p in range(listed):
            tp = rows_ref[p, j] // cls
            both = jnp.concatenate([hi_ref[tp, s, :] for s in picks] + [lo_ref[tp, s, :] for s in picks], axis=0)
            lhi, llo = split(lfull_buf[j, p])
            lead = mm(both, lhi)
            term = lead[:rows] + (lead[rows:] + mm(both[:rows], llo))
            acc = term if acc is None else acc + term
        cov = -acc
        cov_buf[j] = cov.reshape(cov_buf.shape[1:])
        own = lfull_buf[j, :, pl.ds(pl.multiple_of(first, cls), cls), :].reshape(cov.shape)
        put_row(sum_ref, j, jnp.sum(own * cov, axis=0, keepdims=True))

    @pl.loop(0, children // PRODUCT_STEP)
    def _(i):
        group = [i * PRODUCT_STEP + u for u in range(PRODUCT_STEP)]
        for j in group:
            fetch(j).wait()
        for j in group:
            one(j)
        for j in group:
            drain(j).start()

    sums = square_ref[...] - sum_ref[...]
    for i in range(term_ref.shape[0]):
        term_ref[i] = sums

    @pl.loop(0, children)
    def _(j):
        drain(j).wait()


def product(tile_rows, sig, squares, lfull, peers):
    children, listed, depth, out_width = lfull.shape
    width = sig.shape[1]
    tiles = sig.shape[0] * sig.shape[2] // depth
    lines = (2 * children, out_width // 2)
    strips = (children, listed, width // tiles, out_width)
    vmem = pl.BlockSpec(memory_space=pltpu.VMEM)
    smem = pl.BlockSpec(memory_space=pltpu.SMEM)
    hbm = pl.BlockSpec(memory_space=pltpu.HBM)
    return pl.pallas_call(
        product_kernel,
        in_specs=[smem, vmem, vmem, hbm],
        out_specs=[hbm, vmem, vmem],
        out_shape=[
            jax.ShapeDtypeStruct(strips, F32),
            jax.ShapeDtypeStruct((peers,) + lines, F32),
            jax.ShapeDtypeStruct((tiles, width // tiles), F32),
        ],
        scratch_shapes=[
            pltpu.VMEM((tiles, depth), F32),
            pltpu.VMEM((tiles, width, depth), BF16),
            pltpu.VMEM((tiles, width, depth), BF16),
            pltpu.VMEM(lfull.shape, F32),
            pltpu.VMEM(strips, F32),
            pltpu.VMEM(lines, F32),
            pltpu.SemaphoreType.DMA((children,)),
            pltpu.SemaphoreType.DMA((children,)),
        ],
        compiler_params=pltpu.CompilerParams(vmem_limit_bytes=46 << 20),
        name="product",
    )(tile_rows, sig, squares, lfull)


def exchange(value, axis):
    return lax.all_to_all(value, axis, split_axis=0, concat_axis=0, tiled=True)


def spread(value, axis, size):
    return exchange(jnp.broadcast_to(value[None], (size,) + value.shape), axis)


def body(root_inverse, panel, diag_inverse, tile_rows):
    local_rows, tile_count, class_width = root_inverse.shape
    tile_width = panel.shape[3]
    width = tile_count * class_width
    far, near = LEAF["far"], LEAF["near"] * LEAF["x"]
    block = ("near", "x")
    col = tuple(COL)
    col_count = COL["y"] * COL["core"]
    lhat, squares, flat = scale(panel, diag_inverse, root_inverse.transpose(1, 2, 0), near)
    lfull = lax.all_gather(lhat, col, axis=2, tiled=True)
    band_rows = near * local_rows
    share = tile_count // near
    flat, start = lax.optimization_barrier((flat, lax.axis_index(block) * share))
    bands = exchange(flat, block)
    squares = jnp.where(lax.axis_index(col) == 0, squares, 0.0)
    bands, squares, picked = lax.optimization_barrier((bands, squares, tile_rows.T * class_width))
    band = bands.reshape(band_rows, width).T.reshape(tile_count, class_width, band_rows)
    mine = lax.dynamic_slice_in_dim(band, start, share, 0)
    quarter = lax.all_gather(mine, col, axis=1, tiled=True)
    partial = jnp.einsum(
        "ur,kr->uk",
        band.reshape(width, band_rows),
        quarter.reshape(share * tile_width, band_rows),
        precision=lax.Precision.HIGHEST,
        preferred_element_type=F32,
    )
    piece = jnp.sum(exchange(partial.reshape(far, width // far, share * tile_width), "far"), axis=0)
    sig = spread(spread(piece, "far", far), block, near).reshape(near, width, share * tile_width)
    covariance, terms, root_variance = product(picked, sig, squares, lfull, col_count)
    halves = jnp.sum(exchange(terms, col), axis=0)
    count = diag_inverse.shape[0]
    variance = jnp.concatenate([halves[:count], halves[count:]], axis=1)
    return root_variance, covariance, variance


def solution(mesh):
    sizes = {**LEAF, **COL}
    fine = Mesh(mesh.devices.reshape(tuple(sizes.values())), tuple(sizes))
    leaf, col = tuple(LEAF), tuple(COL)
    in_specs = (P(leaf, None, col), P(leaf, None, col, None), P(leaf, None, None), P(leaf, None))
    out_specs = (P(None, col), P(leaf, None, col, None), P(leaf, None))
    return jax.shard_map(body, mesh=fine, in_specs=in_specs, out_specs=out_specs, check_vma=False)
```

```python
import jax
import jax.numpy as jnp
from jax import lax
from jax.experimental import pallas as pl
from jax.experimental.pallas import tpu as pltpu
from jax.sharding import Mesh
from jax.sharding import PartitionSpec as P

F32 = jnp.float32
BF16 = jnp.bfloat16
SCALE_STEP = 4
PRODUCT_STEP = 1
LEAF = {"far": 4, "near": 2, "x": 4}
COL = {"y": 8, "core": 2}


def split(x):
    hi = x.astype(BF16)
    lo = (x - hi.astype(F32)).astype(BF16)
    return hi, lo


def mm(a, b):
    return jnp.dot(a, b, preferred_element_type=F32)


def put_row(ref, j, row):
    count, half = ref.shape[0] // 2, ref.shape[1]
    ref[pl.ds(j, 1), :] = row[:, :half]
    ref[pl.ds(j + count, 1), :] = row[:, half:]


def scale_kernel(panel_hbm, inverse_hbm, lhat_hbm, panel_buf, inverse_buf, lhat_buf, in_sem, out_sem):
    children = inverse_buf.shape[0]
    rows = panel_buf.shape[1] * panel_buf.shape[2]
    half = inverse_buf.shape[1] // 2
    top, low, left = pl.ds(0, half), pl.ds(half, half), pl.ds(0, half)
    groups = children // SCALE_STEP

    def some(i):
        return pl.ds(i * SCALE_STEP, SCALE_STEP)

    def fetch(i):
        return (
            pltpu.make_async_copy(panel_hbm.at[some(i)], panel_buf.at[some(i)], in_sem.at[0, i]),
            pltpu.make_async_copy(inverse_hbm.at[some(i), top, left], inverse_buf.at[some(i), top, left], in_sem.at[1, i]),
            pltpu.make_async_copy(inverse_hbm.at[some(i), low, :], inverse_buf.at[some(i), low, :], in_sem.at[2, i]),
        )

    def drain(i):
        return pltpu.make_async_copy(lhat_buf.at[some(i)], lhat_hbm.at[some(i)], out_sem.at[i])

    for i in range(groups):
        for copy in fetch(i):
            copy.start()

    def one(j):
        first, second = inverse_buf[j, top, left], inverse_buf[j, low, :]
        fhi, flo = split(first)
        shi, slo = split(second)
        phi, plo = split(panel_buf[j].reshape(rows, 2 * half))
        pair = jnp.concatenate([phi, plo], axis=0)
        upper = mm(pair[:, :half], fhi)
        lower = mm(pair[:, half:], shi)
        upper = upper[:rows] + (upper[rows:] + mm(phi[:, :half], flo))
        lower = lower[:rows] + (lower[rows:] + mm(phi[:, half:], slo))
        lhat = jnp.concatenate([lower[:, :half] + upper, lower[:, half:]], axis=1)
        lhat_buf[j] = lhat.reshape(lhat_buf.shape[1:])

    @pl.loop(0, groups)
    def _(i):
        for copy in fetch(i):
            copy.wait()
        for u in range(SCALE_STEP):
            one(i * SCALE_STEP + u)
        drain(i).start()

    for i in range(groups):
        drain(i).wait()


def scale(panel, inverse):
    groups = panel.shape[0] // SCALE_STEP
    hbm = pl.BlockSpec(memory_space=pltpu.HBM)
    return pl.pallas_call(
        scale_kernel,
        in_specs=[hbm, hbm],
        out_specs=hbm,
        out_shape=jax.ShapeDtypeStruct(panel.shape, F32),
        scratch_shapes=[
            pltpu.VMEM(panel.shape, F32),
            pltpu.VMEM(inverse.shape, F32),
            pltpu.VMEM(panel.shape, F32),
            pltpu.SemaphoreType.DMA((3, groups)),
            pltpu.SemaphoreType.DMA((groups,)),
        ],
        name="scale",
    )(panel, inverse)


def square_kernel(inverse_hbm, square_ref, inverse_buf, sem):
    groups = sem.shape[1]
    step = inverse_buf.shape[0] // groups
    half = inverse_buf.shape[1] // 2
    top, low, left = pl.ds(0, half), pl.ds(half, half), pl.ds(0, half)

    def fetch(i):
        some = pl.ds(i * step, step)
        return (
            pltpu.make_async_copy(inverse_hbm.at[some, top, left], inverse_buf.at[some, top, left], sem.at[0, i]),
            pltpu.make_async_copy(inverse_hbm.at[some, low, :], inverse_buf.at[some, low, :], sem.at[1, i]),
        )

    for i in range(groups):
        for copy in fetch(i):
            copy.start()

    @pl.loop(0, groups)
    def _(i):
        for copy in fetch(i):
            copy.wait()
        for u in range(step):
            first, second = inverse_buf[i * step + u, top, left], inverse_buf[i * step + u, low, :]
            before = jnp.sum(first * first, axis=0, keepdims=True)
            squares = jnp.sum(second * second, axis=0, keepdims=True)
            total = jnp.concatenate([squares[:, :half] + before, squares[:, half:]], axis=1)
            put_row(square_ref, i * step + u, total)


def square(inverse):
    children, _, wide = inverse.shape
    return pl.pallas_call(
        square_kernel,
        in_specs=[pl.BlockSpec(memory_space=pltpu.HBM)],
        out_specs=pl.BlockSpec(memory_space=pltpu.VMEM),
        out_shape=jax.ShapeDtypeStruct((2 * children, wide // 2), F32),
        scratch_shapes=[
            pltpu.VMEM(inverse.shape, F32),
            pltpu.SemaphoreType.DMA((2, children // SCALE_STEP)),
        ],
        compiler_params=pltpu.CompilerParams(vmem_limit_bytes=54 << 20),
        name="square",
    )(inverse)


def prepare_kernel(sig_ref, hi_ref, lo_ref, root_ref, diag_ref):
    tiles, width, depth = hi_ref.shape
    cls = width // tiles
    share = sig_ref.shape[2] // depth
    first = (lax.axis_index("y") * COL["core"] + lax.axis_index("core")) * cls
    lane = lax.broadcasted_iota(jnp.int32, (cls, depth), 1)
    row = lax.broadcasted_iota(jnp.int32, (cls, depth), 0)
    on_diag = lane == row + first
    for p in range(tiles):
        part, place = divmod(p, share)
        block = sig_ref[part, :, place * depth : (place + 1) * depth]
        hi, lo = split(block)
        hi_ref[p] = hi
        lo_ref[p] = lo
        own = block[p * cls : (p + 1) * cls]
        diag_ref[p : p + 1, :] = jnp.sum(jnp.where(on_diag, own, 0.0), axis=0, keepdims=True)
    root_ref[...] = pltpu.roll(diag_ref[...], lax.rem(depth - first, depth), 1)[:, :cls]


def prepare(sig, depth):
    width = sig.shape[1]
    tiles = sig.shape[0] * sig.shape[2] // depth
    vmem = pl.BlockSpec(memory_space=pltpu.VMEM)
    return pl.pallas_call(
        prepare_kernel,
        in_specs=[vmem],
        out_specs=[vmem, vmem, vmem],
        out_shape=[
            jax.ShapeDtypeStruct((tiles, width, depth), BF16),
            jax.ShapeDtypeStruct((tiles, width, depth), BF16),
            jax.ShapeDtypeStruct((tiles, width // tiles), F32),
        ],
        scratch_shapes=[pltpu.VMEM((tiles, depth), F32)],
        compiler_params=pltpu.CompilerParams(vmem_limit_bytes=8 << 20),
        name="prepare",
    )(sig)


def product_kernel(rows_ref, hi_ref, lo_ref, square_ref, lfull_hbm, cov_hbm, term_ref, lfull_buf, cov_buf, sum_ref, in_sem, out_sem):
    children, listed, depth, out_width = lfull_buf.shape
    tiles, width, _ = hi_ref.shape
    cls = width // tiles

    def fetch(j):
        return pltpu.make_async_copy(lfull_hbm.at[j], lfull_buf.at[j], in_sem.at[j])

    def drain(j):
        return pltpu.make_async_copy(cov_buf.at[j], cov_hbm.at[j], out_sem.at[j])

    @pl.loop(0, children)
    def _(j):
        fetch(j).start()

    first = (lax.axis_index("y") * COL["core"] + lax.axis_index("core")) * cls

    def one(j):
        picks = [pl.ds(pl.multiple_of(rows_ref[q, j], cls), cls) for q in range(listed)]
        rows = listed * cls
        acc = None
        for p in range(listed):
            tp = rows_ref[p, j] // cls
            both = jnp.concatenate([hi_ref[tp, s, :] for s in picks] + [lo_ref[tp, s, :] for s in picks], axis=0)
            lhi, llo = split(lfull_buf[j, p])
            lead = mm(both, lhi)
            term = lead[:rows] + (lead[rows:] + mm(both[:rows], llo))
            acc = term if acc is None else acc + term
        cov = -acc
        cov_buf[j] = cov.reshape(cov_buf.shape[1:])
        own = lfull_buf[j, :, pl.ds(pl.multiple_of(first, cls), cls), :].reshape(cov.shape)
        put_row(sum_ref, j, jnp.sum(own * cov, axis=0, keepdims=True))

    @pl.loop(0, children // PRODUCT_STEP)
    def _(i):
        group = [i * PRODUCT_STEP + u for u in range(PRODUCT_STEP)]
        for j in group:
            fetch(j).wait()
        for j in group:
            one(j)
        for j in group:
            drain(j).start()

    sums = square_ref[...] - sum_ref[...]
    for i in range(term_ref.shape[0]):
        term_ref[i] = sums

    @pl.loop(0, children)
    def _(j):
        drain(j).wait()


def product(tile_rows, hi, lo, squares, lfull, peers):
    children, listed, depth, out_width = lfull.shape
    tiles, width, _ = hi.shape
    lines = (2 * children, out_width // 2)
    strips = (children, listed, width // tiles, out_width)
    vmem = pl.BlockSpec(memory_space=pltpu.VMEM)
    smem = pl.BlockSpec(memory_space=pltpu.SMEM)
    hbm = pl.BlockSpec(memory_space=pltpu.HBM)
    return pl.pallas_call(
        product_kernel,
        in_specs=[smem, vmem, vmem, vmem, hbm],
        out_specs=[hbm, vmem],
        out_shape=[
            jax.ShapeDtypeStruct(strips, F32),
            jax.ShapeDtypeStruct((peers,) + lines, F32),
        ],
        scratch_shapes=[
            pltpu.VMEM(lfull.shape, F32),
            pltpu.VMEM(strips, F32),
            pltpu.VMEM(lines, F32),
            pltpu.SemaphoreType.DMA((children,)),
            pltpu.SemaphoreType.DMA((children,)),
        ],
        compiler_params=pltpu.CompilerParams(vmem_limit_bytes=46 << 20),
        name="product",
    )(tile_rows, hi, lo, squares, lfull)


def exchange(value, axis):
    return lax.all_to_all(value, axis, split_axis=0, concat_axis=0, tiled=True)


def spread(value, axis, size):
    return exchange(jnp.broadcast_to(value[None], (size,) + value.shape), axis)


def body(root_inverse, panel, diag_inverse, tile_rows):
    local_rows, tile_count, class_width = root_inverse.shape
    tile_width = panel.shape[3]
    width = tile_count * class_width
    far, near = LEAF["far"], LEAF["near"] * LEAF["x"]
    block = ("near", "x")
    col = tuple(COL)
    col_count = COL["y"] * COL["core"]
    lhat = scale(panel, diag_inverse)
    lfull = lax.all_gather(lhat, col, axis=2, tiled=True)
    band_rows = near * local_rows
    share = tile_count // near
    root_late, inverse_late, _ = lax.optimization_barrier((root_inverse, diag_inverse, lhat))
    flat = jnp.broadcast_to(root_late.reshape(local_rows, width)[None], (near, local_rows, width))
    flat, start = lax.optimization_barrier((flat, lax.axis_index(block) * share))
    bands = exchange(flat, block)
    squares = jnp.where(lax.axis_index(col) == 0, square(inverse_late), 0.0)
    bands, squares, picked = lax.optimization_barrier((bands, squares, tile_rows.T * class_width))
    band = bands.reshape(band_rows, width).T.reshape(tile_count, class_width, band_rows)
    mine = lax.dynamic_slice_in_dim(band, start, share, 0)
    quarter = lax.all_gather(mine, col, axis=1, tiled=True)
    partial = jnp.einsum(
        "ur,kr->uk",
        band.reshape(width, band_rows),
        quarter.reshape(share * tile_width, band_rows),
        precision=lax.Precision.HIGHEST,
        preferred_element_type=F32,
    )
    piece = jnp.sum(exchange(partial.reshape(far, width // far, share * tile_width), "far"), axis=0)
    sig = spread(spread(piece, "far", far), block, near).reshape(near, width, share * tile_width)
    hi, lo, root_variance = prepare(sig, tile_width)
    covariance, terms = product(picked, hi, lo, squares, lfull, col_count)
    halves = jnp.sum(exchange(terms, col), axis=0)
    count = diag_inverse.shape[0]
    variance = jnp.concatenate([halves[:count], halves[count:]], axis=1)
    return root_variance, covariance, variance


def solution(mesh):
    sizes = {**LEAF, **COL}
    fine = Mesh(mesh.devices.reshape(tuple(sizes.values())), tuple(sizes))
    leaf, col = tuple(LEAF), tuple(COL)
    in_specs = (P(leaf, None, col), P(leaf, None, col, None), P(leaf, None, None), P(leaf, None))
    out_specs = (P(None, col), P(leaf, None, col, None), P(leaf, None))
    return jax.shard_map(body, mesh=fine, in_specs=in_specs, out_specs=out_specs, check_vma=False)
```

```python
import jax
import jax.numpy as jnp
from jax import lax
from jax.experimental import pallas as pl
from jax.experimental.pallas import tpu as pltpu
from jax.sharding import Mesh
from jax.sharding import PartitionSpec as P

F32 = jnp.float32
BF16 = jnp.bfloat16
SCALE_STEP = 4
LEAF = {"far": 4, "near": 2, "x": 4}
COL = {"y": 8, "core": 2}


def split(x):
    hi = x.astype(BF16)
    lo = (x - hi.astype(F32)).astype(BF16)
    return hi, lo


def mm(a, b):
    return jnp.dot(a, b, preferred_element_type=F32)


def put_row(ref, j, row):
    count, half = ref.shape[0] // 2, ref.shape[1]
    ref[pl.ds(j, 1), :] = row[:, :half]
    ref[pl.ds(j + count, 1), :] = row[:, half:]


def scale_kernel(panel_hbm, inverse_hbm, lhat_hbm, panel_buf, inverse_buf, lhat_buf, in_sem, out_sem):
    children = inverse_buf.shape[0]
    rows = panel_buf.shape[1] * panel_buf.shape[2]
    half = inverse_buf.shape[1] // 2
    top, low, left = pl.ds(0, half), pl.ds(half, half), pl.ds(0, half)
    groups = children // SCALE_STEP

    def some(i):
        return pl.ds(i * SCALE_STEP, SCALE_STEP)

    def fetch(i):
        return (
            pltpu.make_async_copy(panel_hbm.at[some(i)], panel_buf.at[some(i)], in_sem.at[0, i]),
            pltpu.make_async_copy(inverse_hbm.at[some(i), top, left], inverse_buf.at[some(i), top, left], in_sem.at[1, i]),
            pltpu.make_async_copy(inverse_hbm.at[some(i), low, :], inverse_buf.at[some(i), low, :], in_sem.at[2, i]),
        )

    def drain(i):
        return pltpu.make_async_copy(lhat_buf.at[some(i)], lhat_hbm.at[some(i)], out_sem.at[i])

    for i in range(groups):
        for copy in fetch(i):
            copy.start()

    def one(j):
        first, second = inverse_buf[j, top, left], inverse_buf[j, low, :]
        fhi, flo = split(first)
        shi, slo = split(second)
        phi, plo = split(panel_buf[j].reshape(rows, 2 * half))
        pair = jnp.concatenate([phi, plo], axis=0)
        upper = mm(pair[:, :half], fhi)
        lower = mm(pair[:, half:], shi)
        upper = upper[:rows] + (upper[rows:] + mm(phi[:, :half], flo))
        lower = lower[:rows] + (lower[rows:] + mm(phi[:, half:], slo))
        lhat = jnp.concatenate([lower[:, :half] + upper, lower[:, half:]], axis=1)
        lhat_buf[j] = lhat.reshape(lhat_buf.shape[1:])

    @pl.loop(0, groups)
    def _(i):
        for copy in fetch(i):
            copy.wait()
        for u in range(SCALE_STEP):
            one(i * SCALE_STEP + u)
        drain(i).start()

    for i in range(groups):
        drain(i).wait()


def scale(panel, inverse):
    groups = panel.shape[0] // SCALE_STEP
    hbm = pl.BlockSpec(memory_space=pltpu.HBM)
    return pl.pallas_call(
        scale_kernel,
        in_specs=[hbm, hbm],
        out_specs=hbm,
        out_shape=jax.ShapeDtypeStruct(panel.shape, F32),
        scratch_shapes=[
            pltpu.VMEM(panel.shape, F32),
            pltpu.VMEM(inverse.shape, F32),
            pltpu.VMEM(panel.shape, F32),
            pltpu.SemaphoreType.DMA((3, groups)),
            pltpu.SemaphoreType.DMA((groups,)),
        ],
        name="scale",
    )(panel, inverse)


def square_kernel(inverse_hbm, square_ref, inverse_buf, sem):
    groups = sem.shape[1]
    step = inverse_buf.shape[0] // groups
    half = inverse_buf.shape[1] // 2
    top, low, left = pl.ds(0, half), pl.ds(half, half), pl.ds(0, half)

    def fetch(i):
        some = pl.ds(i * step, step)
        return (
            pltpu.make_async_copy(inverse_hbm.at[some, top, left], inverse_buf.at[some, top, left], sem.at[0, i]),
            pltpu.make_async_copy(inverse_hbm.at[some, low, :], inverse_buf.at[some, low, :], sem.at[1, i]),
        )

    for i in range(groups):
        for copy in fetch(i):
            copy.start()

    @pl.loop(0, groups)
    def _(i):
        for copy in fetch(i):
            copy.wait()
        for u in range(step):
            first, second = inverse_buf[i * step + u, top, left], inverse_buf[i * step + u, low, :]
            before = jnp.sum(first * first, axis=0, keepdims=True)
            squares = jnp.sum(second * second, axis=0, keepdims=True)
            total = jnp.concatenate([squares[:, :half] + before, squares[:, half:]], axis=1)
            put_row(square_ref, i * step + u, total)


def square(inverse):
    children, _, wide = inverse.shape
    return pl.pallas_call(
        square_kernel,
        in_specs=[pl.BlockSpec(memory_space=pltpu.HBM)],
        out_specs=pl.BlockSpec(memory_space=pltpu.VMEM),
        out_shape=jax.ShapeDtypeStruct((2 * children, wide // 2), F32),
        scratch_shapes=[
            pltpu.VMEM(inverse.shape, F32),
            pltpu.SemaphoreType.DMA((2, children // SCALE_STEP)),
        ],
        compiler_params=pltpu.CompilerParams(vmem_limit_bytes=54 << 20),
        name="square",
    )(inverse)


def prepare_kernel(sig_ref, hi_ref, lo_ref, root_ref, diag_ref):
    tiles, width, depth = hi_ref.shape
    cls = width // tiles
    share = sig_ref.shape[2] // depth
    first = (lax.axis_index("y") * COL["core"] + lax.axis_index("core")) * cls
    lane = lax.broadcasted_iota(jnp.int32, (cls, depth), 1)
    row = lax.broadcasted_iota(jnp.int32, (cls, depth), 0)
    on_diag = lane == row + first
    for p in range(tiles):
        part, place = divmod(p, share)
        block = sig_ref[part, :, place * depth : (place + 1) * depth]
        hi, lo = split(block)
        hi_ref[p] = hi
        lo_ref[p] = lo
        own = block[p * cls : (p + 1) * cls]
        diag_ref[p : p + 1, :] = jnp.sum(jnp.where(on_diag, own, 0.0), axis=0, keepdims=True)
    root_ref[...] = pltpu.roll(diag_ref[...], lax.rem(depth - first, depth), 1)[:, :cls]


def prepare(sig, depth):
    width = sig.shape[1]
    tiles = sig.shape[0] * sig.shape[2] // depth
    vmem = pl.BlockSpec(memory_space=pltpu.VMEM)
    return pl.pallas_call(
        prepare_kernel,
        in_specs=[vmem],
        out_specs=[vmem, vmem, vmem],
        out_shape=[
            jax.ShapeDtypeStruct((tiles, width, depth), BF16),
            jax.ShapeDtypeStruct((tiles, width, depth), BF16),
            jax.ShapeDtypeStruct((tiles, width // tiles), F32),
        ],
        scratch_shapes=[pltpu.VMEM((tiles, depth), F32)],
        compiler_params=pltpu.CompilerParams(vmem_limit_bytes=8 << 20),
        name="prepare",
    )(sig)


def product_kernel(rows_ref, hi_ref, lo_ref, square_ref, lfull_hbm, cov_hbm, term_ref, lfull_buf, cov_buf, sum_ref, in_sem, out_sem):
    children, listed, depth, out_width = lfull_buf.shape
    tiles, width, _ = hi_ref.shape
    cls = width // tiles

    def fetch(j):
        return pltpu.make_async_copy(lfull_hbm.at[j], lfull_buf.at[j], in_sem.at[j])

    def drain(j):
        return pltpu.make_async_copy(cov_buf.at[j], cov_hbm.at[j], out_sem.at[j])

    last = children - 1
    cut = listed // 2

    def tail(part):
        some = pl.ds(part * cut, cut)
        return pltpu.make_async_copy(lfull_hbm.at[last, some], lfull_buf.at[last, some], in_sem.at[last + part])

    @pl.loop(0, last)
    def _(j):
        fetch(j).start()

    for part in range(2):
        tail(part).start()

    first = (lax.axis_index("y") * COL["core"] + lax.axis_index("core")) * cls

    def one(j, split_wait=False):
        picks = [pl.ds(pl.multiple_of(rows_ref[q, j], cls), cls) for q in range(listed)]
        rows = listed * cls
        acc = None
        for p in range(listed):
            if split_wait and p % cut == 0:
                tail(p // cut).wait()
            tp = rows_ref[p, j] // cls
            both = jnp.concatenate([hi_ref[tp, s, :] for s in picks] + [lo_ref[tp, s, :] for s in picks], axis=0)
            lhi, llo = split(lfull_buf[j, p])
            lead = mm(both, lhi)
            term = lead[:rows] + (lead[rows:] + mm(both[:rows], llo))
            acc = term if acc is None else acc + term
        cov = -acc
        cov_buf[j] = cov.reshape(cov_buf.shape[1:])
        own = lfull_buf[j, :, pl.ds(pl.multiple_of(first, cls), cls), :].reshape(cov.shape)
        put_row(sum_ref, j, jnp.sum(own * cov, axis=0, keepdims=True))

    @pl.loop(0, last)
    def _(j):
        fetch(j).wait()
        one(j)
        drain(j).start()

    one(last, True)
    drain(last).start()

    sums = square_ref[...] - sum_ref[...]
    for i in range(term_ref.shape[0]):
        term_ref[i] = sums

    @pl.loop(0, children)
    def _(j):
        drain(j).wait()


def product(tile_rows, hi, lo, squares, lfull, peers):
    children, listed, depth, out_width = lfull.shape
    tiles, width, _ = hi.shape
    lines = (2 * children, out_width // 2)
    strips = (children, listed, width // tiles, out_width)
    vmem = pl.BlockSpec(memory_space=pltpu.VMEM)
    smem = pl.BlockSpec(memory_space=pltpu.SMEM)
    hbm = pl.BlockSpec(memory_space=pltpu.HBM)
    return pl.pallas_call(
        product_kernel,
        in_specs=[smem, vmem, vmem, vmem, hbm],
        out_specs=[hbm, vmem],
        out_shape=[
            jax.ShapeDtypeStruct(strips, F32),
            jax.ShapeDtypeStruct((peers,) + lines, F32),
        ],
        scratch_shapes=[
            pltpu.VMEM(lfull.shape, F32),
            pltpu.VMEM(strips, F32),
            pltpu.VMEM(lines, F32),
            pltpu.SemaphoreType.DMA((children + 1,)),
            pltpu.SemaphoreType.DMA((children,)),
        ],
        compiler_params=pltpu.CompilerParams(vmem_limit_bytes=46 << 20),
        name="product",
    )(tile_rows, hi, lo, squares, lfull)


def exchange(value, axis):
    return lax.all_to_all(value, axis, split_axis=0, concat_axis=0, tiled=True)


def spread(value, axis, size):
    return exchange(jnp.broadcast_to(value[None], (size,) + value.shape), axis)


def body(root_inverse, panel, diag_inverse, tile_rows):
    local_rows, tile_count, class_width = root_inverse.shape
    tile_width = panel.shape[3]
    width = tile_count * class_width
    far, near = LEAF["far"], LEAF["near"] * LEAF["x"]
    block = ("near", "x")
    col = tuple(COL)
    col_count = COL["y"] * COL["core"]
    lhat = scale(panel, diag_inverse)
    lfull = lax.all_gather(lhat, col, axis=2, tiled=True)
    band_rows = near * local_rows
    share = tile_count // near
    root_late, inverse_late, _ = lax.optimization_barrier((root_inverse, diag_inverse, lhat))
    flat = jnp.broadcast_to(root_late.reshape(local_rows, width)[None], (near, local_rows, width))
    flat, start = lax.optimization_barrier((flat, lax.axis_index(block) * share))
    bands = exchange(flat, block)
    squares = jnp.where(lax.axis_index(col) == 0, square(inverse_late), 0.0)
    bands, squares, picked = lax.optimization_barrier((bands, squares, tile_rows.T * class_width))
    band = bands.reshape(band_rows, width).T.reshape(tile_count, class_width, band_rows)
    mine = lax.dynamic_slice_in_dim(band, start, share, 0)
    quarter = lax.all_gather(mine, col, axis=1, tiled=True)
    partial = jnp.einsum(
        "ur,kr->uk",
        band.reshape(width, band_rows),
        quarter.reshape(share * tile_width, band_rows),
        precision=lax.Precision.HIGHEST,
        preferred_element_type=F32,
    )
    piece = jnp.sum(exchange(partial.reshape(far, width // far, share * tile_width), "far"), axis=0)
    sig = spread(spread(piece, "far", far), block, near).reshape(near, width, share * tile_width)
    hi, lo, root_variance = prepare(sig, tile_width)
    covariance, terms = product(picked, hi, lo, squares, lfull, col_count)
    halves = jnp.sum(exchange(terms, col), axis=0)
    count = diag_inverse.shape[0]
    variance = jnp.concatenate([halves[:count], halves[count:]], axis=1)
    return root_variance, covariance, variance


def solution(mesh):
    sizes = {**LEAF, **COL}
    fine = Mesh(mesh.devices.reshape(tuple(sizes.values())), tuple(sizes))
    leaf, col = tuple(LEAF), tuple(COL)
    in_specs = (P(leaf, None, col), P(leaf, None, col, None), P(leaf, None, None), P(leaf, None))
    out_specs = (P(None, col), P(leaf, None, col, None), P(leaf, None))
    return jax.shard_map(body, mesh=fine, in_specs=in_specs, out_specs=out_specs, check_vma=False)
```

```python
import jax
import jax.numpy as jnp
from jax import lax
from jax.experimental import pallas as pl
from jax.experimental.pallas import tpu as pltpu
from jax.sharding import Mesh
from jax.sharding import PartitionSpec as P

F32 = jnp.float32
BF16 = jnp.bfloat16
SCALE_STEP = 4
PRODUCT_STEP = 2
LEAF = {"far": 4, "near": 2, "x": 4}
COL = {"y": 8, "core": 2}


def split(x):
    hi = x.astype(BF16)
    lo = (x - hi.astype(F32)).astype(BF16)
    return hi, lo


def mm(a, b):
    return jnp.dot(a, b, preferred_element_type=F32)


def put_row(ref, j, row):
    count, half = ref.shape[0] // 2, ref.shape[1]
    ref[pl.ds(j, 1), :] = row[:, :half]
    ref[pl.ds(j + count, 1), :] = row[:, half:]


def scale_kernel(panel_hbm, inverse_hbm, lhat_hbm, panel_buf, inverse_buf, lhat_buf, in_sem, out_sem):
    children = inverse_buf.shape[0]
    rows = panel_buf.shape[1] * panel_buf.shape[2]
    half = inverse_buf.shape[1] // 2
    top, low, left = pl.ds(0, half), pl.ds(half, half), pl.ds(0, half)
    groups = children // SCALE_STEP

    def some(i):
        return pl.ds(i * SCALE_STEP, SCALE_STEP)

    def fetch(i):
        return (
            pltpu.make_async_copy(panel_hbm.at[some(i)], panel_buf.at[some(i)], in_sem.at[0, i]),
            pltpu.make_async_copy(inverse_hbm.at[some(i), top, left], inverse_buf.at[some(i), top, left], in_sem.at[1, i]),
            pltpu.make_async_copy(inverse_hbm.at[some(i), low, :], inverse_buf.at[some(i), low, :], in_sem.at[2, i]),
        )

    def drain(i):
        return pltpu.make_async_copy(lhat_buf.at[some(i)], lhat_hbm.at[some(i)], out_sem.at[i])

    for i in range(groups):
        for copy in fetch(i):
            copy.start()

    def one(j):
        first, second = inverse_buf[j, top, left], inverse_buf[j, low, :]
        fhi, flo = split(first)
        shi, slo = split(second)
        phi, plo = split(panel_buf[j].reshape(rows, 2 * half))
        pair = jnp.concatenate([phi, plo], axis=0)
        upper = mm(pair[:, :half], fhi)
        lower = mm(pair[:, half:], shi)
        upper = upper[:rows] + (upper[rows:] + mm(phi[:, :half], flo))
        lower = lower[:rows] + (lower[rows:] + mm(phi[:, half:], slo))
        lhat = jnp.concatenate([lower[:, :half] + upper, lower[:, half:]], axis=1)
        lhat_buf[j] = lhat.reshape(lhat_buf.shape[1:])

    @pl.loop(0, groups)
    def _(i):
        for copy in fetch(i):
            copy.wait()
        for u in range(SCALE_STEP):
            one(i * SCALE_STEP + u)
        drain(i).start()

    for i in range(groups):
        drain(i).wait()


def scale(panel, inverse):
    groups = panel.shape[0] // SCALE_STEP
    hbm = pl.BlockSpec(memory_space=pltpu.HBM)
    return pl.pallas_call(
        scale_kernel,
        in_specs=[hbm, hbm],
        out_specs=hbm,
        out_shape=jax.ShapeDtypeStruct(panel.shape, F32),
        scratch_shapes=[
            pltpu.VMEM(panel.shape, F32),
            pltpu.VMEM(inverse.shape, F32),
            pltpu.VMEM(panel.shape, F32),
            pltpu.SemaphoreType.DMA((3, groups)),
            pltpu.SemaphoreType.DMA((groups,)),
        ],
        name="scale",
    )(panel, inverse)


def square_kernel(inverse_hbm, square_ref, inverse_buf, sem):
    groups = sem.shape[1]
    step = inverse_buf.shape[0] // groups
    half = inverse_buf.shape[1] // 2
    top, low, left = pl.ds(0, half), pl.ds(half, half), pl.ds(0, half)

    def fetch(i):
        some = pl.ds(i * step, step)
        return (
            pltpu.make_async_copy(inverse_hbm.at[some, top, left], inverse_buf.at[some, top, left], sem.at[0, i]),
            pltpu.make_async_copy(inverse_hbm.at[some, low, :], inverse_buf.at[some, low, :], sem.at[1, i]),
        )

    for i in range(groups):
        for copy in fetch(i):
            copy.start()

    @pl.loop(0, groups)
    def _(i):
        for copy in fetch(i):
            copy.wait()
        for u in range(step):
            first, second = inverse_buf[i * step + u, top, left], inverse_buf[i * step + u, low, :]
            before = jnp.sum(first * first, axis=0, keepdims=True)
            squares = jnp.sum(second * second, axis=0, keepdims=True)
            total = jnp.concatenate([squares[:, :half] + before, squares[:, half:]], axis=1)
            put_row(square_ref, i * step + u, total)


def square(inverse):
    children, _, wide = inverse.shape
    return pl.pallas_call(
        square_kernel,
        in_specs=[pl.BlockSpec(memory_space=pltpu.HBM)],
        out_specs=pl.BlockSpec(memory_space=pltpu.VMEM),
        out_shape=jax.ShapeDtypeStruct((2 * children, wide // 2), F32),
        scratch_shapes=[
            pltpu.VMEM(inverse.shape, F32),
            pltpu.SemaphoreType.DMA((2, children // SCALE_STEP)),
        ],
        compiler_params=pltpu.CompilerParams(vmem_limit_bytes=54 << 20),
        name="square",
    )(inverse)


def prepare_kernel(sig_ref, hi_ref, lo_ref, root_ref, diag_ref):
    tiles, width, depth = hi_ref.shape
    cls = width // tiles
    share = sig_ref.shape[2] // depth
    first = (lax.axis_index("y") * COL["core"] + lax.axis_index("core")) * cls
    lane = lax.broadcasted_iota(jnp.int32, (cls, depth), 1)
    row = lax.broadcasted_iota(jnp.int32, (cls, depth), 0)
    on_diag = lane == row + first
    for p in range(tiles):
        part, place = divmod(p, share)
        block = sig_ref[part, :, place * depth : (place + 1) * depth]
        hi, lo = split(block)
        hi_ref[p] = hi
        lo_ref[p] = lo
        own = block[p * cls : (p + 1) * cls]
        diag_ref[p : p + 1, :] = jnp.sum(jnp.where(on_diag, own, 0.0), axis=0, keepdims=True)
    root_ref[...] = pltpu.roll(diag_ref[...], lax.rem(depth - first, depth), 1)[:, :cls]


def prepare(sig, depth):
    width = sig.shape[1]
    tiles = sig.shape[0] * sig.shape[2] // depth
    vmem = pl.BlockSpec(memory_space=pltpu.VMEM)
    return pl.pallas_call(
        prepare_kernel,
        in_specs=[vmem],
        out_specs=[vmem, vmem, vmem],
        out_shape=[
            jax.ShapeDtypeStruct((tiles, width, depth), BF16),
            jax.ShapeDtypeStruct((tiles, width, depth), BF16),
            jax.ShapeDtypeStruct((tiles, width // tiles), F32),
        ],
        scratch_shapes=[pltpu.VMEM((tiles, depth), F32)],
        compiler_params=pltpu.CompilerParams(vmem_limit_bytes=8 << 20),
        name="prepare",
    )(sig)


def product_kernel(rows_ref, hi_ref, lo_ref, square_ref, lfull_hbm, cov_hbm, term_ref, lfull_buf, cov_buf, sum_ref, in_sem, out_sem):
    children, listed, depth, out_width = lfull_buf.shape
    tiles, width, _ = hi_ref.shape
    cls = width // tiles

    def fetch(j):
        return pltpu.make_async_copy(lfull_hbm.at[j], lfull_buf.at[j], in_sem.at[j])

    def drain(j):
        return pltpu.make_async_copy(cov_buf.at[j], cov_hbm.at[j], out_sem.at[j])

    @pl.loop(0, children)
    def _(j):
        fetch(j).start()

    first = (lax.axis_index("y") * COL["core"] + lax.axis_index("core")) * cls

    def one(j):
        picks = [pl.ds(pl.multiple_of(rows_ref[q, j], cls), cls) for q in range(listed)]
        rows = listed * cls
        acc = None
        for p in range(listed):
            tp = rows_ref[p, j] // cls
            both = jnp.concatenate([hi_ref[tp, s, :] for s in picks] + [lo_ref[tp, s, :] for s in picks], axis=0)
            lhi, llo = split(lfull_buf[j, p])
            lead = mm(both, lhi)
            term = lead[:rows] + (lead[rows:] + mm(both[:rows], llo))
            acc = term if acc is None else acc + term
        cov = -acc
        cov_buf[j] = cov.reshape(cov_buf.shape[1:])
        own = lfull_buf[j, :, pl.ds(pl.multiple_of(first, cls), cls), :].reshape(cov.shape)
        put_row(sum_ref, j, jnp.sum(own * cov, axis=0, keepdims=True))

    @pl.loop(0, children // PRODUCT_STEP)
    def _(i):
        group = [i * PRODUCT_STEP + u for u in range(PRODUCT_STEP)]
        for j in group:
            fetch(j).wait()
        for j in group:
            one(j)
        for j in group:
            drain(j).start()

    sums = square_ref[...] - sum_ref[...]
    for i in range(term_ref.shape[0]):
        term_ref[i] = sums

    @pl.loop(0, children)
    def _(j):
        drain(j).wait()


def product(tile_rows, hi, lo, squares, lfull, peers):
    children, listed, depth, out_width = lfull.shape
    tiles, width, _ = hi.shape
    lines = (2 * children, out_width // 2)
    strips = (children, listed, width // tiles, out_width)
    vmem = pl.BlockSpec(memory_space=pltpu.VMEM)
    smem = pl.BlockSpec(memory_space=pltpu.SMEM)
    hbm = pl.BlockSpec(memory_space=pltpu.HBM)
    return pl.pallas_call(
        product_kernel,
        in_specs=[smem, vmem, vmem, vmem, hbm],
        out_specs=[hbm, vmem],
        out_shape=[
            jax.ShapeDtypeStruct(strips, F32),
            jax.ShapeDtypeStruct((peers,) + lines, F32),
        ],
        scratch_shapes=[
            pltpu.VMEM(lfull.shape, F32),
            pltpu.VMEM(strips, F32),
            pltpu.VMEM(lines, F32),
            pltpu.SemaphoreType.DMA((children,)),
            pltpu.SemaphoreType.DMA((children,)),
        ],
        compiler_params=pltpu.CompilerParams(vmem_limit_bytes=46 << 20),
        name="product",
    )(tile_rows, hi, lo, squares, lfull)


def exchange(value, axis):
    return lax.all_to_all(value, axis, split_axis=0, concat_axis=0, tiled=True)


def spread(value, axis, size):
    return exchange(jnp.broadcast_to(value[None], (size,) + value.shape), axis)


def body(root_inverse, panel, diag_inverse, tile_rows):
    local_rows, tile_count, class_width = root_inverse.shape
    tile_width = panel.shape[3]
    width = tile_count * class_width
    far, near = LEAF["far"], LEAF["near"] * LEAF["x"]
    block = ("near", "x")
    col = tuple(COL)
    col_count = COL["y"] * COL["core"]
    lhat = scale(panel, diag_inverse)
    lfull = lax.all_gather(lhat, col, axis=2, tiled=True)
    band_rows = near * local_rows
    share = tile_count // near
    root_late, inverse_late, _ = lax.optimization_barrier((root_inverse, diag_inverse, lhat))
    flat = jnp.broadcast_to(root_late.reshape(local_rows, width)[None], (near, local_rows, width))
    flat, start = lax.optimization_barrier((flat, lax.axis_index(block) * share))
    bands = exchange(flat, block)
    squares = jnp.where(lax.axis_index(col) == 0, square(inverse_late), 0.0)
    bands, squares, picked = lax.optimization_barrier((bands, squares, tile_rows.T * class_width))
    band = bands.reshape(band_rows, width).T.reshape(tile_count, class_width, band_rows)
    mine = lax.dynamic_slice_in_dim(band, start, share, 0)
    quarter = lax.all_gather(mine, col, axis=1, tiled=True)
    partial = jnp.einsum(
        "ur,kr->uk",
        band.reshape(width, band_rows),
        quarter.reshape(share * tile_width, band_rows),
        precision=lax.Precision.HIGHEST,
        preferred_element_type=F32,
    )
    piece = jnp.sum(exchange(partial.reshape(far, width // far, share * tile_width), "far"), axis=0)
    sig = spread(spread(piece, "far", far), block, near).reshape(near, width, share * tile_width)
    hi, lo, root_variance = prepare(sig, tile_width)
    covariance, terms = product(picked, hi, lo, squares, lfull, col_count)
    halves = jnp.sum(exchange(terms, col), axis=0)
    count = diag_inverse.shape[0]
    variance = jnp.concatenate([halves[:count], halves[count:]], axis=1)
    return root_variance, covariance, variance


def solution(mesh):
    sizes = {**LEAF, **COL}
    fine = Mesh(mesh.devices.reshape(tuple(sizes.values())), tuple(sizes))
    leaf, col = tuple(LEAF), tuple(COL)
    in_specs = (P(leaf, None, col), P(leaf, None, col, None), P(leaf, None, None), P(leaf, None))
    out_specs = (P(None, col), P(leaf, None, col, None), P(leaf, None))
    return jax.shard_map(body, mesh=fine, in_specs=in_specs, out_specs=out_specs, check_vma=False)
```
